32 devices in a mesh: groups: 2 (over x), col: 16 (over z, y, core).
Axes of the slice: x: 2, y: 2, z: 4, core: 2. Of those that a mesh axis runs over, the one named last changes fastest.
Arguments:
- left_features: bfloat16 [32, 8, 8192], P(None, None, ('groups', 'col')), parts along dimension 2, may hold values from -3 to 3
- right_features: bfloat16 [32, 8, 8192], P(None, None, ('groups', 'col')), parts along dimension 2, may hold values from -3 to 3
- tile_offsets: int32 [32], P(('groups', 'col')), parts along dimension 0, may hold values from 0 to 3
- valid_mask: int32 [8, 8192], P(None, ('groups', 'col')), parts along dimension 1, may hold values 0 or 1
Outputs:
- disparity: float32 [8, 8192], P(None, ('groups', 'col')), parts along dimension 1
- final_volume: bfloat16 [192, 8, 8192], P(None, None, ('groups', 'col')), parts along dimension 2
The draws below stay inside these ranges and needn't reach their ends.
There are 2 independent parts, one for each index of `groups`. The reference program is written for one: setup_inputs(seed, part) draws one part's arguments, and reference() takes and returns one part's arrays. A program takes and returns all parts, laid end to end along the dimension named above; each array names one. Nothing has to cross between parts.
All inputs are finite; a program needn't handle non-finite values. No bound on the sum of `valid_mask` on one device may be relied on, other than what follows from the above.
Results may differ from the reference program's by a relative error of at most 0.001.
Values may be sent and summed in bfloat16 or wider, within the bound.
A program may use at most 64 MiB of HBM per device.

```python
import math
import jax
import jax.numpy as jnp
from jax import lax

C = 32
D = 192
W_DEV = 256
ROWS = 8
ITERS = 4
TILES = 16
COLS = 4096


def touch_ends(entries, rng, least, largest):
    place = [jax.random.randint(jax.random.fold_in(rng, axis), (), 0, length) for axis, length in enumerate(entries.shape)]
    longest = entries.shape.index(max(entries.shape))
    neighbour = place[:longest] + [(place[longest] + 1) % entries.shape[longest]] + place[longest + 1:]
    return entries.at[tuple(place)].set(least).at[tuple(neighbour)].set(largest)


def level_of(rng, dims, pieces, least, largest):
    def one(dim, shards_of):
        draws = jax.random.uniform(jax.random.fold_in(jax.random.fold_in(rng, 6), dim), (shards_of,), jnp.float32, least / len(pieces), largest / len(pieces))
        return jnp.repeat(jnp.exp(draws), dims[dim] // shards_of).reshape((-1,) + (1,) * (len(dims) - dim - 1))

    factor_of = one(*pieces[0])
    for cut in pieces[1:]:
        factor_of = factor_of * one(*cut)
    return factor_of


def centred(key, shape, width, most, shards=(), kind=jnp.bfloat16):
    loudness = level_of(key, shape, shards, -0.22, 0.18) if shards else 1.0
    array = jax.random.normal(key, shape, jnp.float32) * width * loudness
    return jnp.minimum(jnp.maximum(array, -most), most).astype(kind)


def setup_inputs(seed: int = 0, part: int = 0) -> dict:
    seeds = jax.random.split(jax.random.key(seed), 5)
    part_keys = jax.random.split(jax.random.fold_in(seeds[4], part), 5)
    left_features = centred(part_keys[0], (C, ROWS, COLS), 1.0, 3.0, ((2, 16),))
    right_features = centred(part_keys[1], (C, ROWS, COLS), 1.0, 3.0, ((2, 16),))
    tile_offsets = touch_ends(jax.random.randint(part_keys[2], (TILES,), 0, 4), jax.random.fold_in(part_keys[2], 1), 0, 3).astype(jnp.int32)
    valid_mask = touch_ends((jax.random.randint(part_keys[3], (ROWS, COLS), 0, 10) < 9).astype(jnp.int32), jax.random.fold_in(part_keys[3], 1), 0, 1)
    return dict(left_features=left_features, right_features=right_features, tile_offsets=tile_offsets, valid_mask=valid_mask)


FLOOR_COST = -4.0
NEIGHBOURS = tuple(((col_step, row_step) for col_step in (-1, 0, 1) for row_step in (-1, 0, 1)))

def affinity(padded, span, tile_rows, channels):
    center = padded[:, 1:1 + tile_rows, 1:1 + span]
    weights = []
    for col_step, row_step in NEIGHBOURS:
        beside = padded[:, 1 + row_step:1 + row_step + tile_rows, 1 + col_step:1 + col_step + span]
        distance = lax.optimization_barrier(jnp.sum((center - beside) ** 2, axis=0))
        weights.append(jnp.exp(-distance / (2.0 * channels)))
    stacked = jnp.stack(weights)
    return stacked / lax.optimization_barrier(jnp.sum(stacked, axis=0, keepdims=True))

def propagate(extended, weights, usable):
    center = extended[:, :, 1:-1]
    tile_rows = center.shape[1]
    span = center.shape[2]
    exponent = jnp.exp(center)
    total = lax.optimization_barrier(jnp.sum(exponent, axis=0))
    purity = center.shape[0] * lax.optimization_barrier(jnp.sum(exponent * exponent, axis=0)) / (total * total)
    gating = purity / (1.0 + purity)
    padded = jnp.pad(extended, ((0, 0), (1, 1), (0, 0)))
    pooled = jnp.zeros(center.shape, jnp.float32)
    for position, (col_step, row_step) in enumerate(NEIGHBOURS):
        beside = padded[:, 1 + row_step:1 + row_step + tile_rows, 1 + col_step:1 + col_step + span]
        pooled = pooled + weights[position][None] * beside
    lower = jnp.concatenate([pooled[:1], pooled[:-1]], axis=0)
    upper = jnp.concatenate([pooled[1:], pooled[-1:]], axis=0)
    smooth = 0.25 * lower + 0.5 * pooled + 0.25 * upper
    return usable[None] * (gating[None] * center + (1.0 - gating[None]) * smooth)

def reference(left_features, right_features, tile_offsets, valid_mask):
    left_float = left_features.astype(jnp.float32)
    right_padded = jnp.pad(right_features.astype(jnp.float32), ((0, 0), (0, 0), (D, 0)))

    def one_disparity(shift):
        moved = lax.dynamic_slice_in_dim(right_padded, (D - shift).astype(jnp.int32), COLS, 2)
        return lax.optimization_barrier(jnp.sum(left_float * moved, axis=0))
    corr = lax.map(one_disparity, jnp.arange(D, dtype=jnp.int32)) / math.sqrt(C)
    columns = jnp.arange(COLS, dtype=jnp.int32)
    tiles = columns // W_DEV
    reach = tile_offsets[tiles]
    shifts = jnp.arange(D, dtype=jnp.int32)
    allowed = columns[None, :] - shifts[:, None] >= (tiles - reach)[None, :] * W_DEV
    usable = valid_mask.astype(jnp.float32)
    volume = jnp.where(allowed[:, None, :], corr, FLOOR_COST) * usable[None]
    padded_guide = jnp.pad(left_float, ((0, 0), (1, 1), (1, 1)))
    weights = affinity(padded_guide, COLS, ROWS, C)
    for turn in range(ITERS):
        extended = jnp.pad(volume, ((0, 0), (0, 0), (1, 1)))
        volume = propagate(extended, weights, usable)
    exponent = jnp.exp(volume)
    probs = exponent / lax.optimization_barrier(jnp.sum(exponent, axis=0, keepdims=True))
    levels = (jnp.arange(D, dtype=jnp.float32) / D)[:, None, None]
    disparity = lax.optimization_barrier(jnp.sum(levels * probs, axis=0))
    return (disparity, volume.astype(jnp.bfloat16))
```

```python
import functools
import math

import jax
import jax.numpy as jnp
from jax import lax
from jax.experimental import pallas as pl
from jax.experimental.pallas import tpu as pltpu
from jax.sharding import PartitionSpec as P

D = 192
ITERS = 4
FLOOR_COST = -4.0
LANES = 128
SUB = 8
MESH = pl.DeviceIdType.MESH
STEPS = tuple((a, b) for a in (-1, 0, 1) for b in (-1, 0, 1))
PITCH = D + 8
GROUP = 32
PER = LANES // GROUP
BLOCKS = D // PER
LOG2E = math.log2(math.e)
FIRST_UNROLL = 48
UNROLL = 192
PUT = 48
STRIP_UNROLL = 48
CHANNEL_UNROLL = 32
VMEM_LIMIT = 24 * 1024 * 1024


def lroll(x, shift):
    shift = shift % x.shape[-1]
    return x if shift == 0 else pltpu.roll(x, shift, x.ndim - 1)


def sroll(x, shift):
    shift = shift % x.shape[-2]
    return x if shift == 0 else pltpu.roll(x, shift, x.ndim - 2)


def iota(shape, dim):
    return lax.broadcasted_iota(jnp.int32, shape, dim)


def distances(plane):
    right = lroll(plane, -1)
    others = (right, sroll(plane, -1), sroll(right, -1), sroll(lroll(plane, 1), -1))
    return tuple((plane - other) ** 2 for other in others) + (plane * plane,)


def affinity(sums, channels):
    across, down, down_right, down_left, norm = sums
    row = iota(across.shape, 0)
    first, last = row == 0, row == across.shape[0] - 1
    dist = {(1, 0): across, (-1, 0): lroll(across, 1)}
    for a, base in ((1, down_right), (0, down), (-1, down_left)):
        dist[a, 1] = jnp.where(last, norm, base)
        dist[-a, -1] = jnp.where(first, norm, sroll(lroll(base, a), 1))
    e = {k: jnp.exp(-d / (2.0 * channels)) for k, d in dist.items()}
    e[0, 0] = jnp.ones_like(across)
    total = sum(e[k] for k in STEPS)
    out = {k: e[k] / total for k in STEPS}
    for a in (-1, 0, 1):
        out[a, 1] = jnp.where(last, 0.0, out[a, 1])
        out[a, -1] = jnp.where(first, 0.0, out[a, -1])
    return out


def coefficients(weights, usable, s1, s2):
    purity = D * s2 / (s1 * s1)
    gating = purity / (1.0 + purity)
    part = 0.25 * usable * (1.0 - gating)
    return {k: lroll(weights[k] * part, k[0]) for k in STEPS}, usable * gating


def columns(w, above, mid, below):
    return [w[a, -1] * above + w[a, 0] * mid + w[a, 1] * below for a in (-1, 0, 1)]


def three(ref, s):
    at = (s + 1) * SUB
    return ref[at - 1 : at - 1 + SUB, :], ref[at : at + SUB, :], ref[at + 1 : at + 1 + SUB, :]


def pack(planes):
    lane = iota((SUB, LANES), 1)
    place = lane % GROUP
    out = jnp.zeros((SUB, LANES), jnp.float32)
    for s, (head, tail) in enumerate(planes):
        mine = lane // GROUP == s
        out = jnp.where(mine & (place >= 4) & (place < 16), lroll(head, GROUP * s + 4), out)
        out = jnp.where(mine & (place >= 16) & (place < 28), lroll(tail, GROUP * s + 16 - 116), out)
    return out


def step(v, st, w_ref, usable, vol_ref, sums, done=None):
    last = vol_ref is not None
    lane = iota((SUB, LANES), 1)
    head_lane, tail_lane = lane == 0, lane == LANES - 1
    none = jnp.zeros((SUB, LANES), jnp.float32)
    wide = lambda a, b: jnp.concatenate([a, b], axis=1)
    w, keep_own = coefficients(
        {k: w_ref[i] for i, k in enumerate(STEPS)}, usable,
        wide(sums[0], sums[2]), wide(sums[1], sums[3]),
    )
    cut = lambda x, t: x[:, t * LANES : (t + 1) * LANES]
    w = [{k: cut(w[k], t) for k in STEPS} for t in range(2)]
    keep_own = [cut(keep_own, t) for t in range(2)]

    def pooled(refs, s):
        z, mid = [], []
        for t in range(2):
            rows = three(refs[t], s)
            mid.append(rows[1])
            z.append(columns(w[t], *rows))
        r = [lroll(z[t][0], 1) for t in range(2)]
        l = [lroll(z[t][2], -1) for t in range(2)]
        r[1] = jnp.where(head_lane, r[0], r[1])
        l[0] = jnp.where(tail_lane, l[1], l[0])
        return [z[t][1] + (r[t] + l[t]) for t in range(2)], mid

    def finish(b, s, pair, sums):
        j = b * UNROLL + s
        pair, sums = list(pair), list(sums)
        if last:
            group = s % PER
            row = pl.multiple_of((b * (UNROLL // PER) + s // PER + 1) * SUB, SUB)
            strip = st[pl.ds(row, SUB), :]
            pair[0] = jnp.where(lane < 4, lroll(strip, -(GROUP * group + 4)), pair[0])
            pair[1] = jnp.where(lane >= LANES - 4, lroll(strip, 100 - GROUP * group), pair[1])
            out = jnp.concatenate(pair, axis=1) * (1.0 / LOG2E)
            vol_ref[D - 1 - j] = out.astype(jnp.bfloat16)
            done(b * UNROLL + s if isinstance(b, int) else s)
            level = (D - 1 - j).astype(jnp.float32) * (1.0 / D)
        for t in range(2):
            if not last:
                v[t, pl.ds(pl.multiple_of((j + 1) * SUB, SUB), SUB), :] = pair[t]
            e = jnp.exp2(pair[t])
            sums[2 * t] += e
            sums[2 * t + 1] += e * (level if last else e)
        return sums

    def advance(refs, b, s, carry):
        p_prev, s_prev, v_prev, acc = carry
        p, mid = pooled(refs, s)
        s_now = [p_prev[t] + p[t] for t in range(2)]
        new = [keep_own[t] * v_prev[t] + (s_prev[t] + s_now[t]) for t in range(2)]
        before = (b - 1, UNROLL - 1) if s == 0 else (b, s - 1)
        return p, s_now, mid, finish(*before, new, acc)

    def block_refs(b):
        at = pl.ds(pl.multiple_of(b * (UNROLL * SUB), SUB), (UNROLL + 2) * SUB)
        return [v.at[t, at, :] for t in range(2)]

    def loop(b, carry):
        p, s, m, acc = carry
        carry = list(p), list(s), list(m), list(acc)
        refs = block_refs(b)
        for k in range(UNROLL):
            carry = advance(refs, b, k, carry)
        return tuple(tuple(c) for c in carry)

    refs = block_refs(0)
    p, mid = pooled(refs, 0)
    carry = p, [2.0 * x for x in p], mid, [none] * 4
    for k in range(1, UNROLL):
        carry = advance(refs, jnp.int32(0), k, carry)
    carry = tuple(tuple(c) for c in carry)
    p_prev, s_prev, v_prev, acc = lax.fori_loop(1, D // UNROLL, loop, carry)
    new = [keep_own[t] * v_prev[t] + (s_prev[t] + 2.0 * p_prev[t]) for t in range(2)]
    return tuple(finish(jnp.int32(D // UNROLL - 1), UNROLL - 1, new, acc))


def kernel(
    n, left_hbm, right_hbm, offs_hbm, mask_hbm, v, st, w_ref, sums_ref, usable_ref,
    left_ref, right_ref, mask_ref, offs_ref,
    prev, lf, rs, t4, part, u, own, sent, from_left, from_right, load_sem, send_sem, recv_sem,
):
    channels = left_ref.shape[0]
    tile = left_ref.shape[2]
    me = lax.axis_index("col")
    has_left, has_right = me > 0, me < n - 1
    lane = iota((SUB, LANES), 1)

    barrier = pltpu.get_barrier_semaphore()

    @pl.when(has_right)
    def _():
        pl.semaphore_signal(barrier, inc=1, device_id={"col": me + 1}, device_id_type=MESH)

    @pl.when(has_left)
    def _():
        pl.semaphore_signal(barrier, inc=1, device_id={"col": me - 1}, device_id_type=MESH)

    loads = [
        pltpu.make_async_copy(src, dst, load_sem.at[i])
        for i, (src, dst) in enumerate((
            (left_hbm, left_ref), (right_hbm, right_ref), (mask_hbm, mask_ref), (offs_hbm, offs_ref)
        ))
    ]
    for load in loads:
        load.start()

    @pl.when(jnp.logical_not(has_left))
    def _():
        prev[...] = jnp.zeros(prev.shape, prev.dtype)
        from_left[...] = jnp.zeros(from_left.shape, jnp.float32)

    @pl.when(jnp.logical_not(has_right))
    def _():
        from_right[...] = jnp.zeros(from_right.shape, jnp.float32)

    def remote(src, dst, slot, to):
        return pltpu.make_async_remote_copy(
            src_ref=src, dst_ref=dst, send_sem=send_sem.at[slot], recv_sem=recv_sem.at[slot],
            device_id={"col": to}, device_id_type=MESH,
        )

    halves = [pl.ds(t * LANES, LANES) for t in range(tile // LANES)]
    tile_copies = [
        remote(right_hbm.at[:, :, half], prev.at[:, :, half], 2 + t, me + 1)
        for t, half in enumerate(halves)
    ]
    strip_right = remote(sent, from_left, 0, me + 1)
    strip_left = remote(sent, from_right, 1, me - 1)

    pl.semaphore_wait(barrier, has_left.astype(jnp.int32) + has_right.astype(jnp.int32))

    @pl.when(has_right)
    def _():
        for copy in tile_copies[::-1]:
            copy.start()

    for load in (loads[0], loads[2]):
        load.wait()

    usable = mask_ref[...].astype(jnp.float32)
    usable_ref[...] = usable

    zero = jnp.zeros((SUB, tile), jnp.float32)

    def channel(c, sums):
        plane = left_ref[c].astype(jnp.float32)
        at = pl.ds(pl.multiple_of(c * SUB, SUB), SUB)
        lf[0, at, :] = plane[:, :LANES]
        lf[1, at, :] = plane[:, LANES:]
        return tuple(s + d for s, d in zip(sums, distances(plane)))

    per = CHANNEL_UNROLL

    def unrolled(body):
        def run(i, carry):
            for k in range(per):
                carry = body(i * per + k, carry)
            return carry

        return run

    weights = affinity(lax.fori_loop(0, channels // per, unrolled(channel), (zero,) * 5), channels)
    for i, k in enumerate(STEPS):
        w_ref[i] = weights[k]

    for q in range(channels // PER):
        planes = [
            (lf[0, (q * PER + s) * SUB : (q * PER + s + 1) * SUB, :],
             lf[1, (q * PER + s) * SUB : (q * PER + s + 1) * SUB, :])
            for s in range(PER)
        ]
        own[BLOCKS + q] = pack(planes)
    mask_at = BLOCKS + channels // PER
    own[mask_at] = pack([(usable[:, :LANES], usable[:, LANES:])] * PER)
    for q in range(mask_at + 1, own.shape[0]):
        own[q] = jnp.zeros((SUB, LANES), jnp.float32)

    loads[1].wait()

    def shifts(source, first, extra):
        def run(c, carry):
            at = pl.ds(pl.multiple_of(c * SUB, SUB), SUB)
            parts = [source[c, :, t * LANES : (t + 1) * LANES].astype(jnp.float32) for t in range(2)]
            if extra is not None:
                parts.append(extra[c, :, :LANES].astype(jnp.float32))
            for s in range(4):
                rolled = [lroll(p, -s) for p in parts]
                for t in range(2):
                    value = rolled[t]
                    if s and t + 1 < len(parts):
                        value = jnp.where(lane < LANES - s, value, rolled[t + 1])
                    rs[s, first + t, at, :] = value
            return carry

        return run

    depth = 8 * channels
    keep = (iota((depth, tile), 0) // channels == iota((depth, tile), 1) % 8).astype(jnp.bfloat16)
    rows_out = tile - 8 + D
    begin = tile - D + 1
    cut = D

    def transposes(y, tiles):
        for t in tiles:
            block = jnp.concatenate(
                [rs[s, t, pl.ds(y, channels, stride=SUB), :] for s in range(4)], axis=0
            )
            t4[y, t * LANES : (t + 1) * LANES, :] = block.T

    def scores_of(y, low, high):
        lhs = jnp.concatenate(
            [t4[y, begin + low : begin + high, :], t4[y, begin + 4 + low : begin + 4 + high, :]],
            axis=1,
        ).astype(jnp.bfloat16)
        l_row = jnp.concatenate(
            [lf[t, pl.ds(y, channels, stride=SUB), :] for t in range(2)], axis=1
        ).astype(jnp.bfloat16)
        rhs = jnp.concatenate([l_row] * 8, axis=0) * keep
        return jnp.dot(lhs, rhs, preferred_element_type=jnp.float32)

    lax.fori_loop(0, channels // per, unrolled(shifts(right_ref, 2, None)), 0)
    for y in range(SUB):
        transposes(y, (2, 3))
    for y in range(SUB):
        part[y] = scores_of(y, cut, rows_out)

    @pl.when(has_left)
    def _():
        for copy in tile_copies[::-1]:
            copy.wait_recv()

    lax.fori_loop(0, channels // per, unrolled(shifts(prev, 0, right_ref)), 0)
    for y in range(SUB):
        transposes(y, (0, 1))
    for y in range(SUB):
        scores = jnp.concatenate([scores_of(y, 0, cut), part[y]], axis=0)
        for t in range(2):
            x = scores[LANES * t : LANES * t + D + LANES - 8, LANES * t : LANES * (t + 1)]
            for bit in (64, 32, 16, 8):
                size = x.shape[0] - bit
                on = (iota((size, LANES), 1) // bit) % 2 == 1
                x = jnp.where(on, x[bit:], x[:size])
            u[t, y * PITCH : y * PITCH + D, :] = x

    loads[3].wait()
    scale = LOG2E / math.sqrt(channels)
    reach = offs_ref[0] * tile
    half = [usable[:, :LANES], usable[:, LANES:]]
    none = jnp.zeros((SUB, LANES), jnp.float32)
    for t in range(2):
        v[t, :SUB, :] = none
        v[t, (D + 1) * SUB :, :] = none
    st[:SUB, :] = none
    st[(BLOCKS + 1) * SUB :, :] = none

    def first(i, sums):
        sums = list(sums)
        for h in range(FIRST_UNROLL):
            b = i * FIRST_UNROLL + h
            planes = []
            for s in range(PER):
                j = b * PER + s
                pair = []
                for t in range(2):
                    corr = u[t, pl.ds(j, SUB, stride=PITCH), :] * scale
                    allowed = lane >= (D - 1 - j) - reach - t * LANES
                    value = jnp.where(allowed, corr, FLOOR_COST * LOG2E) * half[t]
                    v[t, pl.ds(pl.multiple_of((j + 1) * SUB, SUB), SUB), :] = value
                    e = jnp.exp2(value)
                    sums[2 * t] += e
                    sums[2 * t + 1] += e * e
                    pair.append(value)
                planes.append(pair)
            own[b] = pack(planes)
        return tuple(sums)

    sums = lax.fori_loop(0, BLOCKS // FIRST_UNROLL, first, (none,) * 4)

    place4 = (lane % GROUP) // 4
    for m in range(sent.shape[0]):
        out = own[4 * m]
        for s, (p, q) in ((1, (3, 0)), (2, (5, 2)), (3, (7, 4))):
            out = jnp.where((place4 == p) | (place4 == q), lroll(own[4 * m + s], 8 * s), out)
        sent[m] = out

    @pl.when(has_right)
    def _():
        strip_right.start()

    @pl.when(has_left)
    def _():
        strip_left.start()

    sums = lax.fori_loop(
        0, ITERS - 1, lambda i, s: step(v, st, w_ref, usable, None, s), sums
    )

    @pl.when(has_left)
    def _():
        strip_right.wait_recv()

    @pl.when(has_right)
    def _():
        strip_left.wait_recv()

    place = lane % GROUP

    def joined(m, s):
        out = jnp.where(place < 4, lroll(from_left[m], -24 - 8 * s), own[4 * m + s])
        return jnp.where(place >= 28, lroll(from_right[m], 24 - 8 * s), out)

    def over_groups(x):
        x = x + lroll(x, GROUP)
        return x + lroll(x, 2 * GROUP)

    s1, s2 = none, none
    for m in range(BLOCKS // 4):
        for s in range(4):
            value = joined(m, s)
            st[(4 * m + s + 1) * SUB : (4 * m + s + 2) * SUB, :] = value
            e = jnp.exp2(value)
            s1, s2 = s1 + e, s2 + e * e
    strip_sums = (none,) * 5
    for q in range(channels // PER):
        at = BLOCKS + q
        strip_sums = [
            a + d for a, d in zip(strip_sums, distances(joined(at // 4, at % 4)))
        ]
    strip_weights = affinity([over_groups(x) for x in strip_sums], channels)
    strip_usable = joined(mask_at // 4, mask_at % 4)
    low, high = lane < GROUP, lane >= LANES - GROUP

    def strip_step(i, sums):
        w, keep_own = coefficients(
            strip_weights, strip_usable, over_groups(sums[0]), over_groups(sums[1])
        )

        def pooled(ref, s):
            rows = three(ref, s)
            z = columns(w, *rows)
            p = z[1] + (lroll(z[0], 1) + lroll(z[2], -1))
            return p, lroll(p, GROUP), lroll(p, -GROUP), rows[1]

        def finish(b, p, up, before, down, after, value, acc):
            lower, upper = jnp.where(low, before, up), jnp.where(high, after, down)
            new = keep_own * value + ((lower + upper) + 2.0 * p)
            st[pl.ds(pl.multiple_of((b + 1) * SUB, SUB), SUB), :] = new
            e = jnp.exp2(new)
            return acc[0] + e, acc[1] + e * e

        def advance(ref, b, s, carry):
            p, up, down, before, value, acc = carry
            p_now, up_now, down_now, value_now = pooled(ref, s)
            acc = finish(b * STRIP_UNROLL + s - 1, p, up, before, down, down_now, value, acc)
            return p_now, up_now, down_now, up, value_now, acc

        def block_ref(b):
            at = pl.ds(pl.multiple_of(b * (STRIP_UNROLL * SUB), SUB), (STRIP_UNROLL + 2) * SUB)
            return st.at[at, :]

        def loop(b, carry):
            ref = block_ref(b)
            for k in range(STRIP_UNROLL):
                carry = advance(ref, b, k, carry)
            return carry

        ref = block_ref(0)
        p, up, down, value = pooled(ref, 0)
        carry = p, up, down, p, value, (none, none)
        for k in range(1, STRIP_UNROLL):
            carry = advance(ref, jnp.int32(0), k, carry)
        p, up, down, before, value, acc = lax.fori_loop(1, BLOCKS // STRIP_UNROLL, loop, carry)
        return finish(jnp.int32(BLOCKS - 1), p, up, before, down, p, value, acc)

    lax.fori_loop(0, ITERS, strip_step, (s1, s2))

    for t in range(4):
        sums_ref[t] = sums[t]

    @pl.when(has_right)
    def _():
        for copy in tile_copies:
            copy.wait_send()
        strip_right.wait_send()

    @pl.when(has_left)
    def _():
        strip_left.wait_send()


def last_kernel(usable_ref, v, st, w_ref, sums_ref, disp_hbm, vol_hbm, disp_ref, vol_ref, sem):
    def put(b):
        at = pl.ds(D - (b + 1) * PUT, PUT)
        return pltpu.make_async_copy(vol_ref.at[at], vol_hbm.at[at], sem.at[b])

    def done(j):
        if (j + 1) % PUT == 0:
            put(j // PUT).start()

    out = step(v, st, w_ref, usable_ref[...], vol_ref, [sums_ref[t] for t in range(4)], done)
    for t in range(2):
        disp_ref[:, t * LANES : (t + 1) * LANES] = out[2 * t + 1] / out[2 * t]
    disp = pltpu.make_async_copy(disp_ref, disp_hbm, sem.at[D // PUT])
    disp.start()
    for b in range(D // PUT):
        put(b).wait()
    disp.wait()


def on_device(n, left_features, right_features, tile_offsets, valid_mask):
    channels, rows, tile = left_features.shape
    vmem = pl.BlockSpec(memory_space=pltpu.VMEM)
    hbm = pl.BlockSpec(memory_space=pltpu.HBM)
    strips = -(-(BLOCKS + channels // PER + 1) // 4) * 4
    f32 = jnp.float32
    state = pl.pallas_call(
        functools.partial(kernel, n),
        out_shape=(
            jax.ShapeDtypeStruct((2, (D + 2) * SUB, LANES), f32),
            jax.ShapeDtypeStruct(((BLOCKS + 2) * SUB, LANES), f32),
            jax.ShapeDtypeStruct((len(STEPS), SUB, tile), f32),
            jax.ShapeDtypeStruct((4, SUB, LANES), f32),
            jax.ShapeDtypeStruct((SUB, tile), f32),
        ),
        in_specs=[hbm] * 4,
        out_specs=(vmem,) * 5,
        scratch_shapes=[
            pltpu.VMEM((channels, rows, tile), jnp.bfloat16),
            pltpu.VMEM((channels, rows, tile), jnp.bfloat16),
            pltpu.VMEM((rows, tile), jnp.int32),
            pltpu.SMEM((1,), jnp.int32),
            pltpu.VMEM((channels, rows, tile), jnp.bfloat16),
            pltpu.VMEM((2, channels * SUB, LANES), f32),
            pltpu.VMEM((4, 4, channels * SUB, LANES), f32),
            pltpu.VMEM((SUB, 2 * tile, LANES), f32),
            pltpu.VMEM((SUB, tile - 8, tile), f32),
            pltpu.VMEM((2, SUB * PITCH, LANES), f32),
            pltpu.VMEM((strips, SUB, LANES), f32),
            pltpu.VMEM((strips // 4, SUB, LANES), f32),
            pltpu.VMEM((strips // 4, SUB, LANES), f32),
            pltpu.VMEM((strips // 4, SUB, LANES), f32),
            pltpu.SemaphoreType.DMA((4,)),
            pltpu.SemaphoreType.DMA((4,)),
            pltpu.SemaphoreType.DMA((4,)),
        ],
        compiler_params=pltpu.CompilerParams(
            collective_id=0, has_side_effects=True, vmem_limit_bytes=VMEM_LIMIT
        ),
    )(left_features, right_features, tile_offsets, valid_mask)
    v, st, w, sums, usable = state
    return pl.pallas_call(
        last_kernel,
        out_shape=(
            jax.ShapeDtypeStruct((rows, tile), f32),
            jax.ShapeDtypeStruct((D, rows, tile), jnp.bfloat16),
        ),
        in_specs=[vmem] * 5,
        out_specs=(hbm, hbm),
        scratch_shapes=[
            pltpu.VMEM((rows, tile), f32),
            pltpu.VMEM((D, rows, tile), jnp.bfloat16),
            pltpu.SemaphoreType.DMA((D // PUT + 1,)),
        ],
        compiler_params=pltpu.CompilerParams(vmem_limit_bytes=VMEM_LIMIT),
    )(usable, v, st, w, sums)


def solution(mesh):
    return jax.shard_map(
        functools.partial(on_device, mesh.shape["col"]),
        mesh=mesh,
        in_specs=(
            P(None, None, ("groups", "col")),
            P(None, None, ("groups", "col")),
            P(("groups", "col")),
            P(None, ("groups", "col")),
        ),
        out_specs=(P(None, ("groups", "col")), P(None, None, ("groups", "col"))),
        check_vma=False,
    )
```

```python
import functools
import math

import jax
import jax.numpy as jnp
from jax import lax
from jax.experimental import pallas as pl
from jax.experimental.pallas import tpu as pltpu
from jax.sharding import PartitionSpec as P

D = 192
ITERS = 4
FLOOR_COST = -4.0
LANES = 128
SUB = 8
MESH = pl.DeviceIdType.MESH
STEPS = tuple((a, b) for a in (-1, 0, 1) for b in (-1, 0, 1))
PITCH = D + 8
GROUP = 32
PER = LANES // GROUP
BLOCKS = D // PER
LOG2E = math.log2(math.e)
FIRST_UNROLL = 48
UNROLL = 192
PUT = 48
STRIP_UNROLL = 48
CHANNEL_UNROLL = 32
VMEM_LIMIT = 24 * 1024 * 1024


def lroll(x, shift):
    shift = shift % x.shape[-1]
    return x if shift == 0 else pltpu.roll(x, shift, x.ndim - 1)


def sroll(x, shift):
    shift = shift % x.shape[-2]
    return x if shift == 0 else pltpu.roll(x, shift, x.ndim - 2)


def iota(shape, dim):
    return lax.broadcasted_iota(jnp.int32, shape, dim)


def distances(plane):
    right = lroll(plane, -1)
    others = (right, sroll(plane, -1), sroll(right, -1), sroll(lroll(plane, 1), -1))
    return tuple((plane - other) ** 2 for other in others) + (plane * plane,)


def affinity(sums, channels):
    across, down, down_right, down_left, norm = sums
    row = iota(across.shape, 0)
    first, last = row == 0, row == across.shape[0] - 1
    dist = {(1, 0): across, (-1, 0): lroll(across, 1)}
    for a, base in ((1, down_right), (0, down), (-1, down_left)):
        dist[a, 1] = jnp.where(last, norm, base)
        dist[-a, -1] = jnp.where(first, norm, sroll(lroll(base, a), 1))
    e = {k: jnp.exp(-d / (2.0 * channels)) for k, d in dist.items()}
    e[0, 0] = jnp.ones_like(across)
    total = sum(e[k] for k in STEPS)
    out = {k: e[k] / total for k in STEPS}
    for a in (-1, 0, 1):
        out[a, 1] = jnp.where(last, 0.0, out[a, 1])
        out[a, -1] = jnp.where(first, 0.0, out[a, -1])
    return out


def coefficients(weights, usable, s1, s2):
    purity = D * s2 / (s1 * s1)
    gating = purity / (1.0 + purity)
    part = 0.25 * usable * (1.0 - gating)
    return {k: lroll(weights[k] * part, k[0]) for k in STEPS}, usable * gating


def columns(w, above, mid, below):
    return [w[a, -1] * above + w[a, 0] * mid + w[a, 1] * below for a in (-1, 0, 1)]


def three(ref, s):
    at = (s + 1) * SUB
    return ref[at - 1 : at - 1 + SUB, :], ref[at : at + SUB, :], ref[at + 1 : at + 1 + SUB, :]


def pack(planes):
    lane = iota((SUB, LANES), 1)
    place = lane % GROUP
    out = jnp.zeros((SUB, LANES), jnp.float32)
    for s, (head, tail) in enumerate(planes):
        mine = lane // GROUP == s
        out = jnp.where(mine & (place >= 4) & (place < 16), lroll(head, GROUP * s + 4), out)
        out = jnp.where(mine & (place >= 16) & (place < 28), lroll(tail, GROUP * s + 16 - 116), out)
    return out


def step(v, st, w_ref, usable, vol_ref, sums, done=None):
    last = vol_ref is not None
    lane = iota((SUB, LANES), 1)
    head_lane, tail_lane = lane == 0, lane == LANES - 1
    none = jnp.zeros((SUB, LANES), jnp.float32)
    wide = lambda a, b: jnp.concatenate([a, b], axis=1)
    w, keep_own = coefficients(
        {k: w_ref[i] for i, k in enumerate(STEPS)}, usable,
        wide(sums[0], sums[2]), wide(sums[1], sums[3]),
    )
    cut = lambda x, t: x[:, t * LANES : (t + 1) * LANES]
    w = [{k: cut(w[k], t) for k in STEPS} for t in range(2)]
    keep_own = [cut(keep_own, t) for t in range(2)]

    def pooled(refs, s):
        z, mid = [], []
        for t in range(2):
            rows = three(refs[t], s)
            mid.append(rows[1])
            z.append(columns(w[t], *rows))
        r = [lroll(z[t][0], 1) for t in range(2)]
        l = [lroll(z[t][2], -1) for t in range(2)]
        r[1] = jnp.where(head_lane, r[0], r[1])
        l[0] = jnp.where(tail_lane, l[1], l[0])
        return [z[t][1] + (r[t] + l[t]) for t in range(2)], mid

    def finish(b, s, pair, sums):
        j = b * UNROLL + s
        pair, sums = list(pair), list(sums)
        if last:
            group = s % PER
            row = pl.multiple_of((b * (UNROLL // PER) + s // PER + 1) * SUB, SUB)
            strip = st[pl.ds(row, SUB), :]
            pair[0] = jnp.where(lane < 4, lroll(strip, -(GROUP * group + 4)), pair[0])
            pair[1] = jnp.where(lane >= LANES - 4, lroll(strip, 100 - GROUP * group), pair[1])
            out = jnp.concatenate(pair, axis=1) * (1.0 / LOG2E)
            vol_ref[D - 1 - j] = out.astype(jnp.bfloat16)
            done(b * UNROLL + s if isinstance(b, int) else s)
            level = (D - 1 - j).astype(jnp.float32) * (1.0 / D)
        for t in range(2):
            if not last:
                v[t, pl.ds(pl.multiple_of((j + 1) * SUB, SUB), SUB), :] = pair[t]
            e = jnp.exp2(pair[t])
            sums[2 * t] += e
            sums[2 * t + 1] += e * (level if last else e)
        return sums

    def advance(refs, b, s, carry):
        p_prev, s_prev, v_prev, acc = carry
        p, mid = pooled(refs, s)
        s_now = [p_prev[t] + p[t] for t in range(2)]
        new = [keep_own[t] * v_prev[t] + (s_prev[t] + s_now[t]) for t in range(2)]
        before = (b - 1, UNROLL - 1) if s == 0 else (b, s - 1)
        return p, s_now, mid, finish(*before, new, acc)

    def block_refs(b):
        at = pl.ds(pl.multiple_of(b * (UNROLL * SUB), SUB), (UNROLL + 2) * SUB)
        return [v.at[t, at, :] for t in range(2)]

    def loop(b, carry):
        p, s, m, acc = carry
        carry = list(p), list(s), list(m), list(acc)
        refs = block_refs(b)
        for k in range(UNROLL):
            carry = advance(refs, b, k, carry)
        return tuple(tuple(c) for c in carry)

    refs = block_refs(0)
    p, mid = pooled(refs, 0)
    carry = p, [2.0 * x for x in p], mid, [none] * 4
    for k in range(1, UNROLL):
        carry = advance(refs, jnp.int32(0), k, carry)
    carry = tuple(tuple(c) for c in carry)
    p_prev, s_prev, v_prev, acc = lax.fori_loop(1, D // UNROLL, loop, carry)
    new = [keep_own[t] * v_prev[t] + (s_prev[t] + 2.0 * p_prev[t]) for t in range(2)]
    return tuple(finish(jnp.int32(D // UNROLL - 1), UNROLL - 1, new, acc))


def kernel(
    n, left_hbm, right_hbm, mask_hbm, offs_ref, v, st, w_ref, sums_ref, usable_ref,
    left_ref, right_ref, mask_ref,
    prev, lf, rs, t4, part, u, own, sent, from_left, from_right, load_sem, send_sem, recv_sem,
):
    channels = left_ref.shape[0]
    tile = left_ref.shape[2]
    me = lax.axis_index("col")
    has_left, has_right = me > 0, me < n - 1
    lane = iota((SUB, LANES), 1)

    barrier = pltpu.get_barrier_semaphore()

    @pl.when(has_right)
    def _():
        pl.semaphore_signal(barrier, inc=1, device_id={"col": me + 1}, device_id_type=MESH)

    @pl.when(has_left)
    def _():
        pl.semaphore_signal(barrier, inc=1, device_id={"col": me - 1}, device_id_type=MESH)

    loads = [
        pltpu.make_async_copy(src, dst, load_sem.at[i])
        for i, (src, dst) in enumerate((
            (left_hbm, left_ref), (right_hbm, right_ref), (mask_hbm, mask_ref)
        ))
    ]
    for load in loads:
        load.start()

    @pl.when(jnp.logical_not(has_left))
    def _():
        prev[...] = jnp.zeros(prev.shape, prev.dtype)
        from_left[...] = jnp.zeros(from_left.shape, jnp.float32)

    @pl.when(jnp.logical_not(has_right))
    def _():
        from_right[...] = jnp.zeros(from_right.shape, jnp.float32)

    def remote(src, dst, slot, to):
        return pltpu.make_async_remote_copy(
            src_ref=src, dst_ref=dst, send_sem=send_sem.at[slot], recv_sem=recv_sem.at[slot],
            device_id={"col": to}, device_id_type=MESH,
        )

    halves = [pl.ds(t * LANES, LANES) for t in range(tile // LANES)]
    tile_copies = [
        remote(right_hbm.at[:, :, half], prev.at[:, :, half], 2 + t, me + 1)
        for t, half in enumerate(halves)
    ]
    strip_right = remote(sent, from_left, 0, me + 1)
    strip_left = remote(sent, from_right, 1, me - 1)

    pl.semaphore_wait(barrier, has_left.astype(jnp.int32) + has_right.astype(jnp.int32))

    @pl.when(has_right)
    def _():
        for copy in tile_copies[::-1]:
            copy.start()

    for load in (loads[0], loads[2]):
        load.wait()

    usable = mask_ref[...].astype(jnp.float32)
    usable_ref[...] = usable

    zero = jnp.zeros((SUB, tile), jnp.float32)

    def channel(c, sums):
        plane = left_ref[c].astype(jnp.float32)
        at = pl.ds(pl.multiple_of(c * SUB, SUB), SUB)
        lf[0, at, :] = plane[:, :LANES]
        lf[1, at, :] = plane[:, LANES:]
        return tuple(s + d for s, d in zip(sums, distances(plane)))

    per = CHANNEL_UNROLL

    def unrolled(body):
        def run(i, carry):
            for k in range(per):
                carry = body(i * per + k, carry)
            return carry

        return run

    weights = affinity(lax.fori_loop(0, channels // per, unrolled(channel), (zero,) * 5), channels)
    for i, k in enumerate(STEPS):
        w_ref[i] = weights[k]

    for q in range(channels // PER):
        planes = [
            (lf[0, (q * PER + s) * SUB : (q * PER + s + 1) * SUB, :],
             lf[1, (q * PER + s) * SUB : (q * PER + s + 1) * SUB, :])
            for s in range(PER)
        ]
        own[BLOCKS + q] = pack(planes)
    mask_at = BLOCKS + channels // PER
    own[mask_at] = pack([(usable[:, :LANES], usable[:, LANES:])] * PER)
    for q in range(mask_at + 1, own.shape[0]):
        own[q] = jnp.zeros((SUB, LANES), jnp.float32)

    loads[1].wait()

    def shifts(source, first, extra):
        def run(c, carry):
            at = pl.ds(pl.multiple_of(c * SUB, SUB), SUB)
            parts = [source[c, :, t * LANES : (t + 1) * LANES].astype(jnp.float32) for t in range(2)]
            if extra is not None:
                parts.append(extra[c, :, :LANES].astype(jnp.float32))
            for s in range(4):
                rolled = [lroll(p, -s) for p in parts]
                for t in range(2):
                    value = rolled[t]
                    if s and t + 1 < len(parts):
                        value = jnp.where(lane < LANES - s, value, rolled[t + 1])
                    rs[s, first + t, at, :] = value
            return carry

        return run

    depth = 8 * channels
    keep = (iota((depth, tile), 0) // channels == iota((depth, tile), 1) % 8).astype(jnp.bfloat16)
    rows_out = tile - 8 + D
    begin = tile - D + 1
    cut = D

    def transposes(y, tiles):
        for t in tiles:
            block = jnp.concatenate(
                [rs[s, t, pl.ds(y, channels, stride=SUB), :] for s in range(4)], axis=0
            )
            t4[y, t * LANES : (t + 1) * LANES, :] = block.T

    def scores_of(y, low, high):
        lhs = jnp.concatenate(
            [t4[y, begin + low : begin + high, :], t4[y, begin + 4 + low : begin + 4 + high, :]],
            axis=1,
        ).astype(jnp.bfloat16)
        l_row = jnp.concatenate(
            [lf[t, pl.ds(y, channels, stride=SUB), :] for t in range(2)], axis=1
        ).astype(jnp.bfloat16)
        rhs = jnp.concatenate([l_row] * 8, axis=0) * keep
        return jnp.dot(lhs, rhs, preferred_element_type=jnp.float32)

    lax.fori_loop(0, channels // per, unrolled(shifts(right_ref, 2, None)), 0)
    for y in range(SUB):
        transposes(y, (2, 3))
    for y in range(SUB):
        part[y] = scores_of(y, cut, rows_out)

    @pl.when(has_left)
    def _():
        for copy in tile_copies[::-1]:
            copy.wait_recv()

    lax.fori_loop(0, channels // per, unrolled(shifts(prev, 0, right_ref)), 0)
    for y in range(SUB):
        transposes(y, (0, 1))
    for y in range(SUB):
        scores = jnp.concatenate([scores_of(y, 0, cut), part[y]], axis=0)
        for t in range(2):
            x = scores[LANES * t : LANES * t + D + LANES - 8, LANES * t : LANES * (t + 1)]
            for bit in (64, 32, 16, 8):
                size = x.shape[0] - bit
                on = (iota((size, LANES), 1) // bit) % 2 == 1
                x = jnp.where(on, x[bit:], x[:size])
            u[t, y * PITCH : y * PITCH + D, :] = x

    scale = LOG2E / math.sqrt(channels)
    reach = offs_ref[0] * tile
    half = [usable[:, :LANES], usable[:, LANES:]]
    none = jnp.zeros((SUB, LANES), jnp.float32)
    for t in range(2):
        v[t, :SUB, :] = none
        v[t, (D + 1) * SUB :, :] = none
    st[:SUB, :] = none
    st[(BLOCKS + 1) * SUB :, :] = none

    def first(i, sums):
        sums = list(sums)
        for h in range(FIRST_UNROLL):
            b = i * FIRST_UNROLL + h
            planes = []
            for s in range(PER):
                j = b * PER + s
                pair = []
                for t in range(2):
                    corr = u[t, pl.ds(j, SUB, stride=PITCH), :] * scale
                    allowed = lane >= (D - 1 - j) - reach - t * LANES
                    value = jnp.where(allowed, corr, FLOOR_COST * LOG2E) * half[t]
                    v[t, pl.ds(pl.multiple_of((j + 1) * SUB, SUB), SUB), :] = value
                    e = jnp.exp2(value)
                    sums[2 * t] += e
                    sums[2 * t + 1] += e * e
                    pair.append(value)
                planes.append(pair)
            own[b] = pack(planes)
        return tuple(sums)

    sums = lax.fori_loop(0, BLOCKS // FIRST_UNROLL, first, (none,) * 4)

    place4 = (lane % GROUP) // 4
    for m in range(sent.shape[0]):
        out = own[4 * m]
        for s, (p, q) in ((1, (3, 0)), (2, (5, 2)), (3, (7, 4))):
            out = jnp.where((place4 == p) | (place4 == q), lroll(own[4 * m + s], 8 * s), out)
        sent[m] = out

    @pl.when(has_right)
    def _():
        strip_right.start()

    @pl.when(has_left)
    def _():
        strip_left.start()

    sums = lax.fori_loop(
        0, ITERS - 1, lambda i, s: step(v, st, w_ref, usable, None, s), sums
    )

    @pl.when(has_left)
    def _():
        strip_right.wait_recv()

    @pl.when(has_right)
    def _():
        strip_left.wait_recv()

    place = lane % GROUP

    def joined(m, s):
        out = jnp.where(place < 4, lroll(from_left[m], -24 - 8 * s), own[4 * m + s])
        return jnp.where(place >= 28, lroll(from_right[m], 24 - 8 * s), out)

    def over_groups(x):
        x = x + lroll(x, GROUP)
        return x + lroll(x, 2 * GROUP)

    s1, s2 = none, none
    for m in range(BLOCKS // 4):
        for s in range(4):
            value = joined(m, s)
            st[(4 * m + s + 1) * SUB : (4 * m + s + 2) * SUB, :] = value
            e = jnp.exp2(value)
            s1, s2 = s1 + e, s2 + e * e
    strip_sums = (none,) * 5
    for q in range(channels // PER):
        at = BLOCKS + q
        strip_sums = [
            a + d for a, d in zip(strip_sums, distances(joined(at // 4, at % 4)))
        ]
    strip_weights = affinity([over_groups(x) for x in strip_sums], channels)
    strip_usable = joined(mask_at // 4, mask_at % 4)
    low, high = lane < GROUP, lane >= LANES - GROUP

    def strip_step(i, sums):
        w, keep_own = coefficients(
            strip_weights, strip_usable, over_groups(sums[0]), over_groups(sums[1])
        )

        def pooled(ref, s):
            rows = three(ref, s)
            z = columns(w, *rows)
            p = z[1] + (lroll(z[0], 1) + lroll(z[2], -1))
            return p, lroll(p, GROUP), lroll(p, -GROUP), rows[1]

        def finish(b, p, up, before, down, after, value, acc):
            lower, upper = jnp.where(low, before, up), jnp.where(high, after, down)
            new = keep_own * value + ((lower + upper) + 2.0 * p)
            st[pl.ds(pl.multiple_of((b + 1) * SUB, SUB), SUB), :] = new
            e = jnp.exp2(new)
            return acc[0] + e, acc[1] + e * e

        def advance(ref, b, s, carry):
            p, up, down, before, value, acc = carry
            p_now, up_now, down_now, value_now = pooled(ref, s)
            acc = finish(b * STRIP_UNROLL + s - 1, p, up, before, down, down_now, value, acc)
            return p_now, up_now, down_now, up, value_now, acc

        def block_ref(b):
            at = pl.ds(pl.multiple_of(b * (STRIP_UNROLL * SUB), SUB), (STRIP_UNROLL + 2) * SUB)
            return st.at[at, :]

        def loop(b, carry):
            ref = block_ref(b)
            for k in range(STRIP_UNROLL):
                carry = advance(ref, b, k, carry)
            return carry

        ref = block_ref(0)
        p, up, down, value = pooled(ref, 0)
        carry = p, up, down, p, value, (none, none)
        for k in range(1, STRIP_UNROLL):
            carry = advance(ref, jnp.int32(0), k, carry)
        p, up, down, before, value, acc = lax.fori_loop(1, BLOCKS // STRIP_UNROLL, loop, carry)
        return finish(jnp.int32(BLOCKS - 1), p, up, before, down, p, value, acc)

    lax.fori_loop(0, ITERS, strip_step, (s1, s2))

    for t in range(4):
        sums_ref[t] = sums[t]

    @pl.when(has_right)
    def _():
        for copy in tile_copies:
            copy.wait_send()
        strip_right.wait_send()

    @pl.when(has_left)
    def _():
        strip_left.wait_send()


def last_kernel(usable_ref, v, st, w_ref, sums_ref, disp_hbm, vol_hbm, disp_ref, vol_ref, sem):
    def put(b):
        at = pl.ds(D - (b + 1) * PUT, PUT)
        return pltpu.make_async_copy(vol_ref.at[at], vol_hbm.at[at], sem.at[b])

    def done(j):
        if (j + 1) % PUT == 0:
            put(j // PUT).start()

    out = step(v, st, w_ref, usable_ref[...], vol_ref, [sums_ref[t] for t in range(4)], done)
    for t in range(2):
        disp_ref[:, t * LANES : (t + 1) * LANES] = out[2 * t + 1] / out[2 * t]
    disp = pltpu.make_async_copy(disp_ref, disp_hbm, sem.at[D // PUT])
    disp.start()
    for b in range(D // PUT):
        put(b).wait()
    disp.wait()


def on_device(n, left_features, right_features, tile_offsets, valid_mask):
    channels, rows, tile = left_features.shape
    vmem = pl.BlockSpec(memory_space=pltpu.VMEM)
    hbm = pl.BlockSpec(memory_space=pltpu.HBM)
    strips = -(-(BLOCKS + channels // PER + 1) // 4) * 4
    f32 = jnp.float32
    state = pl.pallas_call(
        functools.partial(kernel, n),
        out_shape=(
            jax.ShapeDtypeStruct((2, (D + 2) * SUB, LANES), f32),
            jax.ShapeDtypeStruct(((BLOCKS + 2) * SUB, LANES), f32),
            jax.ShapeDtypeStruct((len(STEPS), SUB, tile), f32),
            jax.ShapeDtypeStruct((4, SUB, LANES), f32),
            jax.ShapeDtypeStruct((SUB, tile), f32),
        ),
        in_specs=[hbm] * 3 + [pl.BlockSpec(memory_space=pltpu.SMEM)],
        out_specs=(vmem,) * 5,
        scratch_shapes=[
            pltpu.VMEM((channels, rows, tile), jnp.bfloat16),
            pltpu.VMEM((channels, rows, tile), jnp.bfloat16),
            pltpu.VMEM((rows, tile), jnp.int32),
            pltpu.VMEM((channels, rows, tile), jnp.bfloat16),
            pltpu.VMEM((2, channels * SUB, LANES), f32),
            pltpu.VMEM((4, 4, channels * SUB, LANES), f32),
            pltpu.VMEM((SUB, 2 * tile, LANES), f32),
            pltpu.VMEM((SUB, tile - 8, tile), f32),
            pltpu.VMEM((2, SUB * PITCH, LANES), f32),
            pltpu.VMEM((strips, SUB, LANES), f32),
            pltpu.VMEM((strips // 4, SUB, LANES), f32),
            pltpu.VMEM((strips // 4, SUB, LANES), f32),
            pltpu.VMEM((strips // 4, SUB, LANES), f32),
            pltpu.SemaphoreType.DMA((3,)),
            pltpu.SemaphoreType.DMA((4,)),
            pltpu.SemaphoreType.DMA((4,)),
        ],
        compiler_params=pltpu.CompilerParams(
            collective_id=0, has_side_effects=True, vmem_limit_bytes=VMEM_LIMIT
        ),
    )(
        *(pltpu.with_memory_space_constraint(x, pltpu.HBM) for x in (left_features, right_features, valid_mask)),
        tile_offsets,
    )
    v, st, w, sums, usable = state
    return pl.pallas_call(
        last_kernel,
        out_shape=(
            jax.ShapeDtypeStruct((rows, tile), f32),
            jax.ShapeDtypeStruct((D, rows, tile), jnp.bfloat16),
        ),
        in_specs=[vmem] * 5,
        out_specs=(hbm, hbm),
        scratch_shapes=[
            pltpu.VMEM((rows, tile), f32),
            pltpu.VMEM((D, rows, tile), jnp.bfloat16),
            pltpu.SemaphoreType.DMA((D // PUT + 1,)),
        ],
        compiler_params=pltpu.CompilerParams(vmem_limit_bytes=VMEM_LIMIT),
    )(usable, v, st, w, sums)


def solution(mesh):
    return jax.shard_map(
        functools.partial(on_device, mesh.shape["col"]),
        mesh=mesh,
        in_specs=(
            P(None, None, ("groups", "col")),
            P(None, None, ("groups", "col")),
            P(("groups", "col")),
            P(None, ("groups", "col")),
        ),
        out_specs=(P(None, ("groups", "col")), P(None, None, ("groups", "col"))),
        check_vma=False,
    )
```

```python
import functools
import math

import jax
import jax.numpy as jnp
from jax import lax
from jax.experimental import pallas as pl
from jax.experimental.pallas import tpu as pltpu
from jax.sharding import PartitionSpec as P

D = 192
ITERS = 4
FLOOR_COST = -4.0
LANES = 128
SUB = 8
MESH = pl.DeviceIdType.MESH
STEPS = tuple((a, b) for a in (-1, 0, 1) for b in (-1, 0, 1))
PITCH = D + 8
GROUP = 32
PER = LANES // GROUP
BLOCKS = D // PER
LOG2E = math.log2(math.e)
FIRST_UNROLL = 48
UNROLL = 192
PUT = 16
CHANNEL_UNROLL = 32
VMEM_LIMIT = 24 * 1024 * 1024


def lroll(x, shift):
    shift = shift % x.shape[-1]
    return x if shift == 0 else pltpu.roll(x, shift, x.ndim - 1)


def sroll(x, shift):
    shift = shift % x.shape[-2]
    return x if shift == 0 else pltpu.roll(x, shift, x.ndim - 2)


def iota(shape, dim):
    return lax.broadcasted_iota(jnp.int32, shape, dim)


def distances(plane):
    right = lroll(plane, -1)
    others = (right, sroll(plane, -1), sroll(right, -1), sroll(lroll(plane, 1), -1))
    return tuple((plane - other) ** 2 for other in others) + (plane * plane,)


def affinity(sums, channels):
    across, down, down_right, down_left, norm = sums
    row = iota(across.shape, 0)
    first, last = row == 0, row == across.shape[0] - 1
    dist = {(1, 0): across, (-1, 0): lroll(across, 1)}
    for a, base in ((1, down_right), (0, down), (-1, down_left)):
        dist[a, 1] = jnp.where(last, norm, base)
        dist[-a, -1] = jnp.where(first, norm, sroll(lroll(base, a), 1))
    e = {k: jnp.exp(-d / (2.0 * channels)) for k, d in dist.items()}
    e[0, 0] = jnp.ones_like(across)
    total = sum(e[k] for k in STEPS)
    out = {k: e[k] / total for k in STEPS}
    for a in (-1, 0, 1):
        out[a, 1] = jnp.where(last, 0.0, out[a, 1])
        out[a, -1] = jnp.where(first, 0.0, out[a, -1])
    return out


def coefficients(weights, usable, s1, s2):
    purity = D * s2 / (s1 * s1)
    gating = purity / (1.0 + purity)
    part = 0.25 * usable * (1.0 - gating)
    return {k: lroll(weights[k] * part, k[0]) for k in STEPS}, usable * gating


def columns(w, above, mid, below):
    return [w[a, -1] * above + w[a, 0] * mid + w[a, 1] * below for a in (-1, 0, 1)]


def three(ref, s):
    at = (s + 1) * SUB
    return ref[at - 1 : at - 1 + SUB, :], ref[at : at + SUB, :], ref[at + 1 : at + 1 + SUB, :]


def pack(planes):
    lane = iota((SUB, LANES), 1)
    place = lane % GROUP
    out = jnp.zeros((SUB, LANES), jnp.float32)
    for s, (head, tail) in enumerate(planes):
        mine = lane // GROUP == s
        out = jnp.where(mine & (place >= 4) & (place < 16), lroll(head, GROUP * s + 4), out)
        out = jnp.where(mine & (place >= 16) & (place < 28), lroll(tail, GROUP * s + 16 - 116), out)
    return out


def step(v, st, w_ref, usable, vol_ref, sums, done=None):
    last = vol_ref is not None
    lane = iota((SUB, LANES), 1)
    head_lane, tail_lane = lane == 0, lane == LANES - 1
    none = jnp.zeros((SUB, LANES), jnp.float32)
    wide = lambda a, b: jnp.concatenate([a, b], axis=1)
    w, keep_own = coefficients(
        {k: w_ref[i] for i, k in enumerate(STEPS)}, usable,
        wide(sums[0], sums[2]), wide(sums[1], sums[3]),
    )
    cut = lambda x, t: x[:, t * LANES : (t + 1) * LANES]
    w = [{k: cut(w[k], t) for k in STEPS} for t in range(2)]
    keep_own = [cut(keep_own, t) for t in range(2)]

    def pooled(refs, s):
        z, mid = [], []
        for t in range(2):
            rows = three(refs[t], s)
            mid.append(rows[1])
            z.append(columns(w[t], *rows))
        r = [lroll(z[t][0], 1) for t in range(2)]
        l = [lroll(z[t][2], -1) for t in range(2)]
        r[1] = jnp.where(head_lane, r[0], r[1])
        l[0] = jnp.where(tail_lane, l[1], l[0])
        return [z[t][1] + (r[t] + l[t]) for t in range(2)], mid

    def finish(b, s, pair, sums):
        j = b * UNROLL + s
        pair, sums = list(pair), list(sums)
        if last:
            group = s // BLOCKS
            strip = st[(s % BLOCKS + 1) * SUB : (s % BLOCKS + 2) * SUB, :]
            pair[0] = jnp.where(lane < 4, lroll(strip, -(GROUP * group + 4)), pair[0])
            pair[1] = jnp.where(lane >= LANES - 4, lroll(strip, 100 - GROUP * group), pair[1])
            out = jnp.concatenate(pair, axis=1) * (1.0 / LOG2E)
            vol_ref[D - 1 - j] = out.astype(jnp.bfloat16)
            done(b * UNROLL + s if isinstance(b, int) else s)
            level = (D - 1 - j).astype(jnp.float32) * (1.0 / D)
        for t in range(2):
            if not last:
                v[t, pl.ds(pl.multiple_of((j + 1) * SUB, SUB), SUB), :] = pair[t]
            e = jnp.exp2(pair[t])
            sums[2 * t] += e
            sums[2 * t + 1] += e * (level if last else e)
        return sums

    def advance(refs, b, s, carry):
        p_prev, s_prev, v_prev, acc = carry
        p, mid = pooled(refs, s)
        s_now = [p_prev[t] + p[t] for t in range(2)]
        new = [keep_own[t] * v_prev[t] + (s_prev[t] + s_now[t]) for t in range(2)]
        before = (b - 1, UNROLL - 1) if s == 0 else (b, s - 1)
        return p, s_now, mid, finish(*before, new, acc)

    def block_refs(b):
        at = pl.ds(pl.multiple_of(b * (UNROLL * SUB), SUB), (UNROLL + 2) * SUB)
        return [v.at[t, at, :] for t in range(2)]

    def loop(b, carry):
        p, s, m, acc = carry
        carry = list(p), list(s), list(m), list(acc)
        refs = block_refs(b)
        for k in range(UNROLL):
            carry = advance(refs, b, k, carry)
        return tuple(tuple(c) for c in carry)

    refs = block_refs(0)
    p, mid = pooled(refs, 0)
    carry = p, [2.0 * x for x in p], mid, [none] * 4
    for k in range(1, UNROLL):
        carry = advance(refs, jnp.int32(0), k, carry)
    carry = tuple(tuple(c) for c in carry)
    p_prev, s_prev, v_prev, acc = lax.fori_loop(1, D // UNROLL, loop, carry)
    new = [keep_own[t] * v_prev[t] + (s_prev[t] + 2.0 * p_prev[t]) for t in range(2)]
    return tuple(finish(jnp.int32(D // UNROLL - 1), UNROLL - 1, new, acc))


def kernel(
    n, left_hbm, right_hbm, mask_hbm, offs_ref, v, st, w_ref, sums_ref, usable_ref,
    left_ref, right_ref, mask_ref,
    high, low_out, low_in, lf, rs, t4, rhs_ref, part, u, own, sent, from_left, from_right, load_sem, send_sem, recv_sem,
):
    channels = left_ref.shape[0]
    tile = left_ref.shape[2]
    me = lax.axis_index("col")
    has_left, has_right = me > 0, me < n - 1
    lane = iota((SUB, LANES), 1)

    barrier = pltpu.get_barrier_semaphore()

    @pl.when(has_right)
    def _():
        pl.semaphore_signal(barrier, inc=1, device_id={"col": me + 1}, device_id_type=MESH)

    @pl.when(has_left)
    def _():
        pl.semaphore_signal(barrier, inc=1, device_id={"col": me - 1}, device_id_type=MESH)

    loads = [
        pltpu.make_async_copy(src, dst, load_sem.at[i])
        for i, (src, dst) in enumerate((
            (left_hbm, left_ref), (right_hbm, right_ref), (mask_hbm, mask_ref)
        ))
    ]
    for load in loads:
        load.start()

    @pl.when(jnp.logical_not(has_left))
    def _():
        high[...] = jnp.zeros(high.shape, high.dtype)
        low_in[...] = jnp.zeros(low_in.shape, low_in.dtype)
        from_left[...] = jnp.zeros(from_left.shape, jnp.float32)

    @pl.when(jnp.logical_not(has_right))
    def _():
        from_right[...] = jnp.zeros(from_right.shape, jnp.float32)

    def remote(src, dst, slot, to):
        return pltpu.make_async_remote_copy(
            src_ref=src, dst_ref=dst, send_sem=send_sem.at[slot], recv_sem=recv_sem.at[slot],
            device_id={"col": to}, device_id_type=MESH,
        )

    high_copy = remote(right_hbm.at[:, :, pl.ds(LANES, LANES)], high, 2, me + 1)
    low_copy = remote(low_out, low_in, 3, me + 1)
    strip_right = remote(sent, from_left, 0, me + 1)
    strip_left = remote(sent, from_right, 1, me - 1)

    pl.semaphore_wait(barrier, has_left.astype(jnp.int32) + has_right.astype(jnp.int32))

    @pl.when(has_right)
    def _():
        high_copy.start()

    loads[1].wait()
    half = channels // 2
    for c in range(half):
        lead = right_ref[c, :, :LANES].astype(jnp.float32)
        trail = right_ref[c + half, :, :LANES].astype(jnp.float32)
        low_out[c] = jnp.where(lane < LANES // 2, lroll(lead, LANES // 2), trail).astype(low_out.dtype)

    for load in (loads[0], loads[2]):
        load.wait()

    usable = mask_ref[...].astype(jnp.float32)
    usable_ref[...] = usable

    zero = jnp.zeros((SUB, tile), jnp.float32)

    def channel(c, sums):
        plane = left_ref[c].astype(jnp.float32)
        at = pl.ds(pl.multiple_of(c * SUB, SUB), SUB)
        lf[0, at, :] = plane[:, :LANES]
        lf[1, at, :] = plane[:, LANES:]
        return tuple(s + d for s, d in zip(sums, distances(plane)))

    per = CHANNEL_UNROLL

    def unrolled(body):
        def run(i, carry):
            for k in range(per):
                carry = body(i * per + k, carry)
            return carry

        return run

    weights = affinity(lax.fori_loop(0, channels // per, unrolled(channel), (zero,) * 5), channels)
    for i, k in enumerate(STEPS):
        w_ref[i] = weights[k]

    for q in range(channels // PER):
        planes = [
            (lf[0, (q * PER + s) * SUB : (q * PER + s + 1) * SUB, :],
             lf[1, (q * PER + s) * SUB : (q * PER + s + 1) * SUB, :])
            for s in range(PER)
        ]
        own[BLOCKS + q] = pack(planes)
    @pl.when(has_right)
    def _():
        low_copy.start()

    mask_at = BLOCKS + channels // PER
    own[mask_at] = pack([(usable[:, :LANES], usable[:, LANES:])] * PER)
    for q in range(mask_at + 1, own.shape[0]):
        own[q] = jnp.zeros((SUB, LANES), jnp.float32)

    def own_part(t):
        return lambda c: right_ref[c, :, t * LANES : (t + 1) * LANES].astype(jnp.float32)

    def high_part(c):
        return high[c].astype(jnp.float32)

    def low_part(c):
        x = low_in[c % half].astype(jnp.float32)
        return lroll(x, LANES // 2) if c < half else x

    def shifts(t, part_of, next_of):
        for c in range(channels):
            now = part_of(c)
            after = now if next_of is None else next_of(c)
            for s in range(4):
                value = lroll(jnp.where(lane < s, after, now), -s) if s else now
                rs[s, t, c * SUB : (c + 1) * SUB, :] = value

    depth = 8 * channels
    keep = (iota((depth, tile), 0) // channels == iota((depth, tile), 1) % 8).astype(jnp.bfloat16)
    rows_out = tile - 8 + D
    begin = tile - D + 1
    first_cut, second_cut = LANES // 2, D

    def transposes(t):
        for y in range(SUB):
            block = jnp.concatenate(
                [rs[s, t, pl.ds(y, channels, stride=SUB), :] for s in range(4)], axis=0
            )
            t4[y, t * LANES : (t + 1) * LANES, :] = block.T

    def scores_of(y, low, high, width):
        lhs = jnp.concatenate(
            [t4[y, begin + low : begin + high, :], t4[y, begin + 4 + low : begin + 4 + high, :]],
            axis=1,
        ).astype(jnp.bfloat16)
        return jnp.dot(lhs, rhs_ref[y, :, :width], preferred_element_type=jnp.float32)

    def straighten(y, t, x):
        for bit in (64, 32, 16, 8):
            size = x.shape[0] - bit
            on = (iota((size, LANES), 1) // bit) % 2 == 1
            x = jnp.where(on, x[bit:], x[:size])
        u[t, y * PITCH : y * PITCH + D, :] = x

    shifts(2, own_part(0), own_part(1))
    shifts(3, own_part(1), None)
    transposes(2)
    transposes(3)
    for y in range(SUB):
        l_row = jnp.concatenate(
            [lf[t, pl.ds(y, channels, stride=SUB), :] for t in range(2)], axis=1
        ).astype(jnp.bfloat16)
        rhs_ref[y] = jnp.concatenate([l_row] * 8, axis=0) * keep
        part[y, second_cut:, :] = scores_of(y, second_cut, rows_out, tile)

    @pl.when(has_left)
    def _():
        high_copy.wait_recv()

    shifts(1, high_part, own_part(0))
    transposes(1)
    for y in range(SUB):
        part[y, first_cut:second_cut, :] = scores_of(y, first_cut, second_cut, tile)
        straighten(y, 1, part[y, LANES:, LANES:])

    @pl.when(has_left)
    def _():
        low_copy.wait_recv()

    shifts(0, low_part, high_part)
    transposes(0)
    for y in range(SUB):
        x = scores_of(y, 0, first_cut, LANES)
        straighten(y, 0, jnp.concatenate([x, part[y, first_cut : D + LANES - 8, :LANES]], axis=0))

    scale = LOG2E / math.sqrt(channels)
    reach = offs_ref[0] * tile
    half = [usable[:, :LANES], usable[:, LANES:]]
    none = jnp.zeros((SUB, LANES), jnp.float32)
    for t in range(2):
        v[t, :SUB, :] = none
        v[t, (D + 1) * SUB :, :] = none
    st[:SUB, :] = none
    st[(BLOCKS + 1) * SUB :, :] = none

    def first(i, sums):
        sums = list(sums)
        for h in range(FIRST_UNROLL):
            b = i * FIRST_UNROLL + h
            planes = []
            for s in range(PER):
                j = s * BLOCKS + b
                pair = []
                for t in range(2):
                    corr = u[t, pl.ds(j, SUB, stride=PITCH), :] * scale
                    allowed = lane >= (D - 1 - j) - reach - t * LANES
                    value = jnp.where(allowed, corr, FLOOR_COST * LOG2E) * half[t]
                    v[t, pl.ds(pl.multiple_of((j + 1) * SUB, SUB), SUB), :] = value
                    e = jnp.exp2(value)
                    sums[2 * t] += e
                    sums[2 * t + 1] += e * e
                    pair.append(value)
                planes.append(pair)
            own[b] = pack(planes)
        return tuple(sums)

    sums = lax.fori_loop(0, BLOCKS // FIRST_UNROLL, first, (none,) * 4)

    place4 = (lane % GROUP) // 4
    for m in range(sent.shape[0]):
        out = own[4 * m]
        for s, (p, q) in ((1, (3, 0)), (2, (5, 2)), (3, (7, 4))):
            out = jnp.where((place4 == p) | (place4 == q), lroll(own[4 * m + s], 8 * s), out)
        sent[m] = out

    @pl.when(has_right)
    def _():
        strip_right.start()

    @pl.when(has_left)
    def _():
        strip_left.start()

    sums = lax.fori_loop(
        0, ITERS - 1, lambda i, s: step(v, st, w_ref, usable, None, s), sums
    )

    @pl.when(has_left)
    def _():
        strip_right.wait_recv()

    @pl.when(has_right)
    def _():
        strip_left.wait_recv()

    place = lane % GROUP

    def joined(m, s):
        out = jnp.where(place < 4, lroll(from_left[m], -24 - 8 * s), own[4 * m + s])
        return jnp.where(place >= 28, lroll(from_right[m], 24 - 8 * s), out)

    def over_groups(x):
        x = x + lroll(x, GROUP)
        return x + lroll(x, 2 * GROUP)

    s1, s2 = none, none
    for m in range(BLOCKS // 4):
        for s in range(4):
            value = joined(m, s)
            st[(4 * m + s + 1) * SUB : (4 * m + s + 2) * SUB, :] = value
            e = jnp.exp2(value)
            s1, s2 = s1 + e, s2 + e * e
    strip_sums = (none,) * 5
    for q in range(channels // PER):
        at = BLOCKS + q
        strip_sums = [
            a + d for a, d in zip(strip_sums, distances(joined(at // 4, at % 4)))
        ]
    strip_weights = affinity([over_groups(x) for x in strip_sums], channels)
    strip_usable = joined(mask_at // 4, mask_at % 4)
    lowest, highest = lane < GROUP, lane >= LANES - GROUP

    def strip_step(i, sums):
        w, keep_own = coefficients(
            strip_weights, strip_usable, over_groups(sums[0]), over_groups(sums[1])
        )

        def pooled(b):
            rows = three(st, b)
            z = columns(w, *rows)
            return z[1] + (lroll(z[0], 1) + lroll(z[2], -1)), rows[1]

        p, value = pooled(0)
        p_end, value_end = pooled(BLOCKS - 1)
        pair = p + jnp.where(lowest, p, lroll(p_end, GROUP))
        p_after = jnp.where(highest, p_end, lroll(p, -GROUP))
        s1, s2 = none, none
        for b in range(BLOCKS):
            if b < BLOCKS - 2:
                p_now, value_now = pooled(b + 1)
            elif b == BLOCKS - 2:
                p_now, value_now = p_end, value_end
            else:
                p_now, value_now = p_after, None
            pair_now = p + p_now
            new = keep_own * value + (pair + pair_now)
            st[(b + 1) * SUB : (b + 2) * SUB, :] = new
            e = jnp.exp2(new)
            s1, s2 = s1 + e, s2 + e * e
            p, value, pair = p_now, value_now, pair_now
        return s1, s2

    lax.fori_loop(0, ITERS, strip_step, (s1, s2))

    for t in range(4):
        sums_ref[t] = sums[t]

    @pl.when(has_right)
    def _():
        high_copy.wait_send()
        low_copy.wait_send()
        strip_right.wait_send()

    @pl.when(has_left)
    def _():
        strip_left.wait_send()


def last_kernel(usable_ref, v, st, w_ref, sums_ref, disp_hbm, vol_hbm, disp_ref, vol_ref, sem):
    def put(b):
        at = pl.ds(D - (b + 1) * PUT, PUT)
        return pltpu.make_async_copy(vol_ref.at[at], vol_hbm.at[at], sem.at[b])

    def done(j):
        if (j + 1) % PUT == 0:
            put(j // PUT).start()

    out = step(v, st, w_ref, usable_ref[...], vol_ref, [sums_ref[t] for t in range(4)], done)
    for t in range(2):
        disp_ref[:, t * LANES : (t + 1) * LANES] = out[2 * t + 1] / out[2 * t]
    disp = pltpu.make_async_copy(disp_ref, disp_hbm, sem.at[D // PUT])
    disp.start()
    for b in range(D // PUT):
        put(b).wait()
    disp.wait()


def on_device(n, left_features, right_features, tile_offsets, valid_mask):
    channels, rows, tile = left_features.shape
    vmem = pl.BlockSpec(memory_space=pltpu.VMEM)
    hbm = pl.BlockSpec(memory_space=pltpu.HBM)
    strips = -(-(BLOCKS + channels // PER + 1) // 4) * 4
    f32 = jnp.float32
    state = pl.pallas_call(
        functools.partial(kernel, n),
        out_shape=(
            jax.ShapeDtypeStruct((2, (D + 2) * SUB, LANES), f32),
            jax.ShapeDtypeStruct(((BLOCKS + 2) * SUB, LANES), f32),
            jax.ShapeDtypeStruct((len(STEPS), SUB, tile), f32),
            jax.ShapeDtypeStruct((4, SUB, LANES), f32),
            jax.ShapeDtypeStruct((SUB, tile), f32),
        ),
        in_specs=[hbm] * 3 + [pl.BlockSpec(memory_space=pltpu.SMEM)],
        out_specs=(vmem,) * 5,
        scratch_shapes=[
            pltpu.VMEM((channels, rows, tile), jnp.bfloat16),
            pltpu.VMEM((channels, rows, tile), jnp.bfloat16),
            pltpu.VMEM((rows, tile), jnp.int32),
            pltpu.VMEM((channels, rows, LANES), jnp.bfloat16),
            pltpu.VMEM((channels // 2, rows, LANES), jnp.bfloat16),
            pltpu.VMEM((channels // 2, rows, LANES), jnp.bfloat16),
            pltpu.VMEM((2, channels * SUB, LANES), f32),
            pltpu.VMEM((4, 4, channels * SUB, LANES), f32),
            pltpu.VMEM((SUB, 2 * tile, LANES), f32),
            pltpu.VMEM((SUB, 8 * channels, tile), jnp.bfloat16),
            pltpu.VMEM((SUB, tile - 8 + D, tile), f32),
            pltpu.VMEM((2, SUB * PITCH, LANES), f32),
            pltpu.VMEM((strips, SUB, LANES), f32),
            pltpu.VMEM((strips // 4, SUB, LANES), f32),
            pltpu.VMEM((strips // 4, SUB, LANES), f32),
            pltpu.VMEM((strips // 4, SUB, LANES), f32),
            pltpu.SemaphoreType.DMA((3,)),
            pltpu.SemaphoreType.DMA((4,)),
            pltpu.SemaphoreType.DMA((4,)),
        ],
        compiler_params=pltpu.CompilerParams(
            collective_id=0, has_side_effects=True, vmem_limit_bytes=VMEM_LIMIT
        ),
    )(
        *(pltpu.with_memory_space_constraint(x, pltpu.HBM) for x in (left_features, right_features, valid_mask)),
        tile_offsets,
    )
    v, st, w, sums, usable = state
    return pl.pallas_call(
        last_kernel,
        out_shape=(
            jax.ShapeDtypeStruct((rows, tile), f32),
            jax.ShapeDtypeStruct((D, rows, tile), jnp.bfloat16),
        ),
        in_specs=[vmem] * 5,
        out_specs=(hbm, hbm),
        scratch_shapes=[
            pltpu.VMEM((rows, tile), f32),
            pltpu.VMEM((D, rows, tile), jnp.bfloat16),
            pltpu.SemaphoreType.DMA((D // PUT + 1,)),
        ],
        compiler_params=pltpu.CompilerParams(vmem_limit_bytes=VMEM_LIMIT),
    )(usable, v, st, w, sums)


def solution(mesh):
    return jax.shard_map(
        functools.partial(on_device, mesh.shape["col"]),
        mesh=mesh,
        in_specs=(
            P(None, None, ("groups", "col")),
            P(None, None, ("groups", "col")),
            P(("groups", "col")),
            P(None, ("groups", "col")),
        ),
        out_specs=(P(None, ("groups", "col")), P(None, None, ("groups", "col"))),
        check_vma=False,
    )
```

```python
import functools
import math

import jax
import jax.numpy as jnp
from jax import lax
from jax.experimental import pallas as pl
from jax.experimental.pallas import tpu as pltpu
from jax.sharding import PartitionSpec as P

D = 192
ITERS = 4
FLOOR_COST = -4.0
LANES = 128
SUB = 8
MESH = pl.DeviceIdType.MESH
STEPS = tuple((a, b) for a in (-1, 0, 1) for b in (-1, 0, 1))
PITCH = D + 8
GROUP = 32
PER = LANES // GROUP
BLOCKS = D // PER
LOG2E = math.log2(math.e)
UNROLL = 192
PUT = 16
CHANNEL_UNROLL = 32
VMEM_LIMIT = 24 * 1024 * 1024


def lroll(x, shift):
    shift = shift % x.shape[-1]
    return x if shift == 0 else pltpu.roll(x, shift, x.ndim - 1)


def sroll(x, shift):
    shift = shift % x.shape[-2]
    return x if shift == 0 else pltpu.roll(x, shift, x.ndim - 2)


def iota(shape, dim):
    return lax.broadcasted_iota(jnp.int32, shape, dim)


def distances(plane):
    right = lroll(plane, -1)
    others = (right, sroll(plane, -1), sroll(right, -1), sroll(lroll(plane, 1), -1))
    return tuple((plane - other) ** 2 for other in others) + (plane * plane,)


def affinity(sums, channels):
    across, down, down_right, down_left, norm = sums
    row = iota(across.shape, 0)
    first, last = row == 0, row == across.shape[0] - 1
    dist = {(1, 0): across, (-1, 0): lroll(across, 1)}
    for a, base in ((1, down_right), (0, down), (-1, down_left)):
        dist[a, 1] = jnp.where(last, norm, base)
        dist[-a, -1] = jnp.where(first, norm, sroll(lroll(base, a), 1))
    e = {k: jnp.exp(-d / (2.0 * channels)) for k, d in dist.items()}
    e[0, 0] = jnp.ones_like(across)
    total = sum(e[k] for k in STEPS)
    out = {k: e[k] / total for k in STEPS}
    for a in (-1, 0, 1):
        out[a, 1] = jnp.where(last, 0.0, out[a, 1])
        out[a, -1] = jnp.where(first, 0.0, out[a, -1])
    return out


def gate(s1, s2):
    purity = D * s2 / (s1 * s1)
    return purity / (1.0 + purity)


def coefficients(weights, usable, s1, s2):
    gating = gate(s1, s2)
    part = 0.25 * usable * (1.0 - gating)
    return {k: lroll(weights[k] * part, k[0]) for k in STEPS}, usable * gating


def columns(w, above, mid, below):
    return [w[a, -1] * above + w[a, 0] * mid + w[a, 1] * below for a in (-1, 0, 1)]


def three(ref, s):
    at = (s + 1) * SUB
    return ref[at - 1 : at - 1 + SUB, :], ref[at : at + SUB, :], ref[at + 1 : at + 1 + SUB, :]


def pack(planes):
    lane = iota((SUB, LANES), 1)
    place = lane % GROUP
    out = jnp.zeros((SUB, LANES), jnp.float32)
    for s, (head, tail) in enumerate(planes):
        mine = lane // GROUP == s
        out = jnp.where(mine & (place >= 4) & (place < 16), lroll(head, GROUP * s + 4), out)
        out = jnp.where(mine & (place >= 16) & (place < 28), lroll(tail, GROUP * s + 16 - 116), out)
    return out


def step(v, st, w_ref, usable, vol_ref, sums, done=None):
    last = vol_ref is not None
    lane = iota((SUB, LANES), 1)
    head_lane, tail_lane = lane == 0, lane == LANES - 1
    none = jnp.zeros((SUB, LANES), jnp.float32)
    wide = lambda a, b: jnp.concatenate([a, b], axis=1)
    w, keep_own = coefficients(
        {k: w_ref[i] for i, k in enumerate(STEPS)}, usable,
        wide(sums[0], sums[2]), wide(sums[1], sums[3]),
    )
    cut = lambda x, t: x[:, t * LANES : (t + 1) * LANES]
    w = [{k: cut(w[k], t) for k in STEPS} for t in range(2)]
    keep_own = [cut(keep_own, t) for t in range(2)]

    def pooled(refs, s):
        z, mid = [], []
        for t in range(2):
            rows = three(refs[t], s)
            mid.append(rows[1])
            z.append(columns(w[t], *rows))
        r = [lroll(z[t][0], 1) for t in range(2)]
        l = [lroll(z[t][2], -1) for t in range(2)]
        r[1] = jnp.where(head_lane, r[0], r[1])
        l[0] = jnp.where(tail_lane, l[1], l[0])
        return [z[t][1] + (r[t] + l[t]) for t in range(2)], mid

    def finish(b, s, pair, sums):
        j = b * UNROLL + s
        pair, sums = list(pair), list(sums)
        if last:
            group = s // BLOCKS
            strip = st[(s % BLOCKS + 1) * SUB : (s % BLOCKS + 2) * SUB, :]
            pair[0] = jnp.where(lane < 4, lroll(strip, -(GROUP * group + 4)), pair[0])
            pair[1] = jnp.where(lane >= LANES - 4, lroll(strip, 100 - GROUP * group), pair[1])
            out = jnp.concatenate(pair, axis=1) * (1.0 / LOG2E)
            vol_ref[D - 1 - j] = out.astype(jnp.bfloat16)
            done(b * UNROLL + s if isinstance(b, int) else s)
            level = (D - 1 - j).astype(jnp.float32) * (1.0 / D)
        for t in range(2):
            if not last:
                v[t, pl.ds(pl.multiple_of((j + 1) * SUB, SUB), SUB), :] = pair[t]
            e = jnp.exp2(pair[t])
            sums[2 * t] += e
            sums[2 * t + 1] += e * (level if last else e)
        return sums

    def advance(refs, b, s, carry):
        p_prev, s_prev, v_prev, acc = carry
        p, mid = pooled(refs, s)
        s_now = [p_prev[t] + p[t] for t in range(2)]
        new = [keep_own[t] * v_prev[t] + (s_prev[t] + s_now[t]) for t in range(2)]
        before = (b - 1, UNROLL - 1) if s == 0 else (b, s - 1)
        return p, s_now, mid, finish(*before, new, acc)

    def block_refs(b):
        at = pl.ds(pl.multiple_of(b * (UNROLL * SUB), SUB), (UNROLL + 2) * SUB)
        return [v.at[t, at, :] for t in range(2)]

    def loop(b, carry):
        p, s, m, acc = carry
        carry = list(p), list(s), list(m), list(acc)
        refs = block_refs(b)
        for k in range(UNROLL):
            carry = advance(refs, b, k, carry)
        return tuple(tuple(c) for c in carry)

    refs = block_refs(0)
    p, mid = pooled(refs, 0)
    carry = p, [2.0 * x for x in p], mid, [none] * 4
    for k in range(1, UNROLL):
        carry = advance(refs, jnp.int32(0), k, carry)
    carry = tuple(tuple(c) for c in carry)
    p_prev, s_prev, v_prev, acc = lax.fori_loop(1, D // UNROLL, loop, carry)
    new = [keep_own[t] * v_prev[t] + (s_prev[t] + 2.0 * p_prev[t]) for t in range(2)]
    return tuple(finish(jnp.int32(D // UNROLL - 1), UNROLL - 1, new, acc))


def kernel(
    n, left_hbm, right_hbm, mask_hbm, offs_ref, v, st, w_ref, sums_ref, usable_ref,
    left_ref, right_ref, mask_ref,
    high, low_out, low_in, lf, rs, t4, rhs_ref, part, u, own, edge_sent, edge_left, edge_right, sent, from_left, from_right, load_sem, send_sem, recv_sem,
):
    channels = left_ref.shape[0]
    tile = left_ref.shape[2]
    me = lax.axis_index("col")
    has_left, has_right = me > 0, me < n - 1
    lane = iota((SUB, LANES), 1)

    barrier = pltpu.get_barrier_semaphore()

    @pl.when(has_right)
    def _():
        pl.semaphore_signal(barrier, inc=1, device_id={"col": me + 1}, device_id_type=MESH)

    @pl.when(has_left)
    def _():
        pl.semaphore_signal(barrier, inc=1, device_id={"col": me - 1}, device_id_type=MESH)

    loads = [
        pltpu.make_async_copy(src, dst, load_sem.at[i])
        for i, (src, dst) in enumerate((
            (right_hbm, right_ref), (left_hbm, left_ref), (mask_hbm, mask_ref)
        ))
    ]
    for load in loads:
        load.start()

    @pl.when(jnp.logical_not(has_left))
    def _():
        high[...] = jnp.zeros(high.shape, high.dtype)
        low_in[...] = jnp.zeros(low_in.shape, low_in.dtype)
        from_left[...] = jnp.zeros(from_left.shape, jnp.float32)
        edge_left[...] = jnp.zeros(edge_left.shape, jnp.float32)

    @pl.when(jnp.logical_not(has_right))
    def _():
        from_right[...] = jnp.zeros(from_right.shape, jnp.float32)
        edge_right[...] = jnp.zeros(edge_right.shape, jnp.float32)

    def remote(src, dst, slot, to):
        return pltpu.make_async_remote_copy(
            src_ref=src, dst_ref=dst, send_sem=send_sem.at[slot], recv_sem=recv_sem.at[slot],
            device_id={"col": to}, device_id_type=MESH,
        )

    high_copy = remote(right_ref.at[:, :, pl.ds(LANES, LANES)], high, 2, me + 1)
    low_copy = remote(low_out, low_in, 3, me + 1)
    strip_right = remote(sent.at[1], from_left, 0, me + 1)
    strip_left = remote(sent.at[0], from_right, 1, me - 1)
    edge_right_copy = remote(edge_sent.at[1], edge_left, 4, me + 1)
    edge_left_copy = remote(edge_sent.at[0], edge_right, 5, me - 1)

    pl.semaphore_wait(barrier, has_left.astype(jnp.int32) + has_right.astype(jnp.int32))

    loads[0].wait()

    @pl.when(has_right)
    def _():
        high_copy.start()

    half = channels // 2
    for c in range(half):
        lead = right_ref[c, :, :LANES].astype(jnp.float32)
        trail = right_ref[c + half, :, :LANES].astype(jnp.float32)
        low_out[c] = jnp.where(lane < LANES // 2, lroll(lead, LANES // 2), trail).astype(low_out.dtype)

    for load in loads[1:]:
        load.wait()

    usable = mask_ref[...].astype(jnp.float32)
    usable_ref[...] = usable

    zero = jnp.zeros((SUB, tile), jnp.float32)

    def channel(c, sums):
        plane = left_ref[c].astype(jnp.float32)
        at = pl.ds(pl.multiple_of(c * SUB, SUB), SUB)
        lf[0, at, :] = plane[:, :LANES]
        lf[1, at, :] = plane[:, LANES:]
        return tuple(s + d for s, d in zip(sums, distances(plane)))

    per = CHANNEL_UNROLL

    def unrolled(body):
        def run(i, carry):
            for k in range(per):
                carry = body(i * per + k, carry)
            return carry

        return run

    weights = affinity(lax.fori_loop(0, channels // per, unrolled(channel), (zero,) * 5), channels)
    for i, k in enumerate(STEPS):
        w_ref[i] = weights[k]

    for q in range(channels // PER):
        planes = [
            (lf[0, (q * PER + s) * SUB : (q * PER + s + 1) * SUB, :],
             lf[1, (q * PER + s) * SUB : (q * PER + s + 1) * SUB, :])
            for s in range(PER)
        ]
        own[BLOCKS + q] = pack(planes)
    @pl.when(has_right)
    def _():
        low_copy.start()

    mask_at = BLOCKS + channels // PER
    own[mask_at] = pack([(usable[:, :LANES], usable[:, LANES:])] * PER)
    for q in range(mask_at + 1, own.shape[0]):
        own[q] = jnp.zeros((SUB, LANES), jnp.float32)

    place4 = (lane % GROUP) // 4

    def gather(first, target):
        for m in range(target.shape[1]):
            for side, at in ((0, 1), (1, 6)):
                out = own[first + 8 * m + at]
                for i in range(8):
                    if i != at:
                        out = jnp.where(place4 == i, lroll(own[first + 8 * m + i], 4 * (i - at)), out)
                target[side, m] = out

    gather(BLOCKS, edge_sent)

    @pl.when(has_right)
    def _():
        edge_right_copy.start()

    @pl.when(has_left)
    def _():
        edge_left_copy.start()

    def own_part(t):
        return lambda c: right_ref[c, :, t * LANES : (t + 1) * LANES].astype(jnp.float32)

    def high_part(c):
        return high[c].astype(jnp.float32)

    def low_part(c):
        x = low_in[c % half].astype(jnp.float32)
        return lroll(x, LANES // 2) if c < half else x

    def shifts(t, part_of, next_of):
        for c in range(channels):
            now = part_of(c)
            after = now if next_of is None else next_of(c)
            for s in range(4):
                value = lroll(jnp.where(lane < s, after, now), -s) if s else now
                rs[s, t, c * SUB : (c + 1) * SUB, :] = value

    depth = 8 * channels
    keep = (iota((depth, tile), 0) // channels == iota((depth, tile), 1) % 8).astype(jnp.bfloat16)
    rows_out = tile - 8 + D
    begin = tile - D + 1
    first_cut, second_cut = LANES // 2, D

    def transposes(t):
        for y in range(SUB):
            block = jnp.concatenate(
                [rs[s, t, pl.ds(y, channels, stride=SUB), :] for s in range(4)], axis=0
            )
            t4[y, t * LANES : (t + 1) * LANES, :] = block.T

    def scores_of(y, low, high, width):
        lhs = jnp.concatenate(
            [t4[y, begin + low : begin + high, :], t4[y, begin + 4 + low : begin + 4 + high, :]],
            axis=1,
        ).astype(jnp.bfloat16)
        return jnp.dot(lhs, rhs_ref[y, :, :width], preferred_element_type=jnp.float32)

    def straighten(y, t, x):
        for bit in (64, 32, 16, 8):
            size = x.shape[0] - bit
            on = (iota((size, LANES), 1) // bit) % 2 == 1
            x = jnp.where(on, x[bit:], x[:size])
        u[t, y * PITCH : y * PITCH + D, :] = x

    shifts(2, own_part(0), own_part(1))
    shifts(3, own_part(1), None)
    transposes(2)
    transposes(3)
    for y in range(SUB):
        l_row = jnp.concatenate(
            [lf[t, pl.ds(y, channels, stride=SUB), :] for t in range(2)], axis=1
        ).astype(jnp.bfloat16)
        rhs_ref[y] = jnp.concatenate([l_row] * 8, axis=0) * keep
        part[y, second_cut:, :] = scores_of(y, second_cut, rows_out, tile)

    @pl.when(has_left)
    def _():
        high_copy.wait_recv()

    shifts(1, high_part, own_part(0))
    transposes(1)
    for y in range(SUB):
        part[y, first_cut:second_cut, :] = scores_of(y, first_cut, second_cut, tile)
        straighten(y, 1, part[y, LANES:, LANES:])

    @pl.when(has_left)
    def _():
        low_copy.wait_recv()

    shifts(0, low_part, high_part)
    transposes(0)
    for y in range(SUB):
        x = scores_of(y, 0, first_cut, LANES)
        straighten(y, 0, jnp.concatenate([x, part[y, first_cut : D + LANES - 8, :LANES]], axis=0))

    scale = LOG2E / math.sqrt(channels)
    reach = offs_ref[0] * tile
    limit = [lane + (reach + t * LANES) for t in range(2)]
    factor = [usable[:, t * LANES : (t + 1) * LANES] * scale for t in range(2)]
    none = jnp.zeros((SUB, LANES), jnp.float32)
    for t in range(2):
        v[t, :SUB, :] = none
        v[t, (D + 1) * SUB :, :] = none
    st[:SUB, :] = none
    st[(BLOCKS + 1) * SUB :, :] = none

    sums = [none] * 4
    for b in range(BLOCKS):
        planes = []
        for s in range(PER):
            j = s * BLOCKS + b
            pair = []
            for t in range(2):
                corr = u[t, pl.ds(j, SUB, stride=PITCH), :]
                value = jnp.where(limit[t] >= D - 1 - j, corr, FLOOR_COST * LOG2E / scale) * factor[t]
                v[t, (j + 1) * SUB : (j + 2) * SUB, :] = value
                e = jnp.exp2(value)
                sums[2 * t] += e
                sums[2 * t + 1] += e * e
                pair.append(value)
            planes.append(pair)
        own[b] = pack(planes)
    sums = tuple(sums)

    gather(0, sent)

    @pl.when(has_right)
    def _():
        strip_right.start()

    @pl.when(has_left)
    def _():
        strip_left.start()

    sums = lax.fori_loop(
        0, ITERS - 1, lambda i, s: step(v, st, w_ref, usable, None, s), sums
    )

    @pl.when(has_left)
    def _():
        edge_right_copy.wait_recv()
        strip_right.wait_recv()

    @pl.when(has_right)
    def _():
        edge_left_copy.wait_recv()
        strip_left.wait_recv()

    def joined(left, right, first, b):
        m, i = divmod(b, 8)
        out = jnp.where(place4 == 0, lroll(left[m], -4 * i), own[first + b])
        return jnp.where(place4 == 7, lroll(right[m], 4 * (7 - i)), out)

    def over_groups(x):
        return (x + lroll(x, GROUP)) + (lroll(x, 2 * GROUP) + lroll(x, 3 * GROUP))

    strip_sums = (none,) * 5
    for q in range(channels // PER):
        strip_sums = [
            a + d for a, d in zip(strip_sums, distances(joined(edge_left, edge_right, BLOCKS, q)))
        ]
    strip_weights = affinity([over_groups(x) for x in strip_sums], channels)
    strip_weights = {k: lroll(strip_weights[k], k[0]) for k in STEPS}
    strip_usable = joined(edge_left, edge_right, BLOCKS, channels // PER)
    s1, s2 = none, none
    for b in range(BLOCKS):
        value = joined(from_left, from_right, 0, b)
        st[(b + 1) * SUB : (b + 2) * SUB, :] = value
        e = jnp.exp2(value)
        s1, s2 = s1 + e, s2 + e * e
    lowest, highest = lane < GROUP, lane >= LANES - GROUP

    def strip_step(i, sums):
        gating = gate(over_groups(sums[0]), over_groups(sums[1]))
        keep_own, part = strip_usable * gating, 0.25 * strip_usable * (1.0 - gating)

        def pooled(b):
            rows = three(st, b)
            z = columns(strip_weights, *rows)
            return z[1] + (lroll(z[0], 1) + lroll(z[2], -1)), rows[1]

        p, value = pooled(0)
        p_end, value_end = pooled(BLOCKS - 1)
        pair = p + jnp.where(lowest, p, lroll(p_end, GROUP))
        p_after = jnp.where(highest, p_end, lroll(p, -GROUP))
        s1, s2 = none, none
        for b in range(BLOCKS):
            if b < BLOCKS - 2:
                p_now, value_now = pooled(b + 1)
            elif b == BLOCKS - 2:
                p_now, value_now = p_end, value_end
            else:
                p_now, value_now = p_after, None
            pair_now = p + p_now
            new = keep_own * value + part * (pair + pair_now)
            st[(b + 1) * SUB : (b + 2) * SUB, :] = new
            e = jnp.exp2(new)
            s1, s2 = s1 + e, s2 + e * e
            p, value, pair = p_now, value_now, pair_now
        return s1, s2

    lax.fori_loop(0, ITERS, strip_step, (s1, s2))

    for t in range(4):
        sums_ref[t] = sums[t]

    @pl.when(has_right)
    def _():
        high_copy.wait_send()
        low_copy.wait_send()
        edge_right_copy.wait_send()
        strip_right.wait_send()

    @pl.when(has_left)
    def _():
        edge_left_copy.wait_send()
        strip_left.wait_send()


def last_kernel(usable_ref, v, st, w_ref, sums_ref, disp_hbm, vol_hbm, disp_ref, vol_ref, sem):
    def put(b):
        at = pl.ds(D - (b + 1) * PUT, PUT)
        return pltpu.make_async_copy(vol_ref.at[at], vol_hbm.at[at], sem.at[b])

    def done(j):
        if (j + 1) % PUT == 0:
            put(j // PUT).start()

    out = step(v, st, w_ref, usable_ref[...], vol_ref, [sums_ref[t] for t in range(4)], done)
    for t in range(2):
        disp_ref[:, t * LANES : (t + 1) * LANES] = out[2 * t + 1] / out[2 * t]
    disp = pltpu.make_async_copy(disp_ref, disp_hbm, sem.at[D // PUT])
    disp.start()
    for b in range(D // PUT):
        put(b).wait()
    disp.wait()


def on_device(n, left_features, right_features, tile_offsets, valid_mask):
    channels, rows, tile = left_features.shape
    vmem = pl.BlockSpec(memory_space=pltpu.VMEM)
    hbm = pl.BlockSpec(memory_space=pltpu.HBM)
    edges = -(-(channels // PER + 1) // 8)
    strips = BLOCKS + 8 * edges
    f32 = jnp.float32
    state = pl.pallas_call(
        functools.partial(kernel, n),
        out_shape=(
            jax.ShapeDtypeStruct((2, (D + 2) * SUB, LANES), f32),
            jax.ShapeDtypeStruct(((BLOCKS + 2) * SUB, LANES), f32),
            jax.ShapeDtypeStruct((len(STEPS), SUB, tile), f32),
            jax.ShapeDtypeStruct((4, SUB, LANES), f32),
            jax.ShapeDtypeStruct((SUB, tile), f32),
        ),
        in_specs=[hbm] * 3 + [pl.BlockSpec(memory_space=pltpu.SMEM)],
        out_specs=(vmem,) * 5,
        scratch_shapes=[
            pltpu.VMEM((channels, rows, tile), jnp.bfloat16),
            pltpu.VMEM((channels, rows, tile), jnp.bfloat16),
            pltpu.VMEM((rows, tile), jnp.int32),
            pltpu.VMEM((channels, rows, LANES), jnp.bfloat16),
            pltpu.VMEM((channels // 2, rows, LANES), jnp.bfloat16),
            pltpu.VMEM((channels // 2, rows, LANES), jnp.bfloat16),
            pltpu.VMEM((2, channels * SUB, LANES), f32),
            pltpu.VMEM((4, 4, channels * SUB, LANES), f32),
            pltpu.VMEM((SUB, 2 * tile, LANES), f32),
            pltpu.VMEM((SUB, 8 * channels, tile), jnp.bfloat16),
            pltpu.VMEM((SUB, tile - 8 + D, tile), f32),
            pltpu.VMEM((2, SUB * PITCH, LANES), f32),
            pltpu.VMEM((strips, SUB, LANES), f32),
            pltpu.VMEM((2, edges, SUB, LANES), f32),
            pltpu.VMEM((edges, SUB, LANES), f32),
            pltpu.VMEM((edges, SUB, LANES), f32),
            pltpu.VMEM((2, BLOCKS // 8, SUB, LANES), f32),
            pltpu.VMEM((BLOCKS // 8, SUB, LANES), f32),
            pltpu.VMEM((BLOCKS // 8, SUB, LANES), f32),
            pltpu.SemaphoreType.DMA((3,)),
            pltpu.SemaphoreType.DMA((6,)),
            pltpu.SemaphoreType.DMA((6,)),
        ],
        compiler_params=pltpu.CompilerParams(
            collective_id=0, has_side_effects=True, vmem_limit_bytes=VMEM_LIMIT
        ),
    )(
        *(pltpu.with_memory_space_constraint(x, pltpu.HBM) for x in (left_features, right_features, valid_mask)),
        tile_offsets,
    )
    v, st, w, sums, usable = state
    return pl.pallas_call(
        last_kernel,
        out_shape=(
            jax.ShapeDtypeStruct((rows, tile), f32),
            jax.ShapeDtypeStruct((D, rows, tile), jnp.bfloat16),
        ),
        in_specs=[vmem] * 5,
        out_specs=(hbm, hbm),
        scratch_shapes=[
            pltpu.VMEM((rows, tile), f32),
            pltpu.VMEM((D, rows, tile), jnp.bfloat16),
            pltpu.SemaphoreType.DMA((D // PUT + 1,)),
        ],
        compiler_params=pltpu.CompilerParams(vmem_limit_bytes=VMEM_LIMIT),
    )(usable, v, st, w, sums)


def solution(mesh):
    return jax.shard_map(
        functools.partial(on_device, mesh.shape["col"]),
        mesh=mesh,
        in_specs=(
            P(None, None, ("groups", "col")),
            P(None, None, ("groups", "col")),
            P(("groups", "col")),
            P(None, ("groups", "col")),
        ),
        out_specs=(P(None, ("groups", "col")), P(None, None, ("groups", "col"))),
        check_vma=False,
    )
```

```python
import functools
import math

import jax
import jax.numpy as jnp
from jax import lax
from jax.experimental import pallas as pl
from jax.experimental.pallas import tpu as pltpu
from jax.sharding import PartitionSpec as P

D = 192
ITERS = 4
FLOOR_COST = -4.0
LANES = 128
SUB = 8
MESH = pl.DeviceIdType.MESH
STEPS = tuple((a, b) for a in (-1, 0, 1) for b in (-1, 0, 1))
PITCH = D + 8
GROUP = 32
PER = LANES // GROUP
BLOCKS = D // PER
LOG2E = math.log2(math.e)
UNROLL = 192
PUT = 16
VMEM_LIMIT = 24 * 1024 * 1024


def lroll(x, shift):
    shift = shift % x.shape[-1]
    return x if shift == 0 else pltpu.roll(x, shift, x.ndim - 1)


def sroll(x, shift):
    shift = shift % x.shape[-2]
    return x if shift == 0 else pltpu.roll(x, shift, x.ndim - 2)


def iota(shape, dim):
    return lax.broadcasted_iota(jnp.int32, shape, dim)


def distances(plane):
    right = lroll(plane, -1)
    others = (right, sroll(plane, -1), sroll(right, -1), sroll(lroll(plane, 1), -1))
    return tuple((plane - other) ** 2 for other in others) + (plane * plane,)


def affinity(sums, channels):
    across, down, down_right, down_left, norm = sums
    row = iota(across.shape, 0)
    first, last = row == 0, row == across.shape[0] - 1
    dist = {(1, 0): across, (-1, 0): lroll(across, 1)}
    for a, base in ((1, down_right), (0, down), (-1, down_left)):
        dist[a, 1] = jnp.where(last, norm, base)
        dist[-a, -1] = jnp.where(first, norm, sroll(lroll(base, a), 1))
    e = {k: jnp.exp(-d / (2.0 * channels)) for k, d in dist.items()}
    e[0, 0] = jnp.ones_like(across)
    total = sum(e[k] for k in STEPS)
    out = {k: e[k] / total for k in STEPS}
    for a in (-1, 0, 1):
        out[a, 1] = jnp.where(last, 0.0, out[a, 1])
        out[a, -1] = jnp.where(first, 0.0, out[a, -1])
    return out


def gate(s1, s2):
    purity = D * s2 / (s1 * s1)
    return purity / (1.0 + purity)


def coefficients(weights, usable, s1, s2):
    gating = gate(s1, s2)
    part = 0.25 * usable * (1.0 - gating)
    return {k: lroll(weights[k] * part, k[0]) for k in STEPS}, usable * gating


def columns(w, above, mid, below):
    return [w[a, -1] * above + w[a, 0] * mid + w[a, 1] * below for a in (-1, 0, 1)]


def three(ref, s):
    at = (s + 1) * SUB
    return ref[at - 1 : at - 1 + SUB, :], ref[at : at + SUB, :], ref[at + 1 : at + 1 + SUB, :]


def pack(planes, side, out):
    lane = iota((SUB, LANES), 1)
    place = lane % GROUP
    low, shift = ((4, 4), (16, 16 - 116))[side]
    here = (place >= low) & (place < low + 12)
    for s, plane in enumerate(planes):
        out = jnp.where((lane // GROUP == s) & here, lroll(plane, GROUP * s + shift), out)
    return out


def step(v, st, w_ref, usable, vol_ref, sums, done=None):
    last = vol_ref is not None
    lane = iota((SUB, LANES), 1)
    head_lane, tail_lane = lane == 0, lane == LANES - 1
    none = jnp.zeros((SUB, LANES), jnp.float32)
    wide = lambda a, b: jnp.concatenate([a, b], axis=1)
    w, keep_own = coefficients(
        {k: w_ref[i] for i, k in enumerate(STEPS)}, usable,
        wide(sums[0], sums[2]), wide(sums[1], sums[3]),
    )
    cut = lambda x, t: x[:, t * LANES : (t + 1) * LANES]
    w = [{k: cut(w[k], t) for k in STEPS} for t in range(2)]
    keep_own = [cut(keep_own, t) for t in range(2)]

    def pooled(refs, s):
        z, mid = [], []
        for t in range(2):
            rows = three(refs[t], s)
            mid.append(rows[1])
            z.append(columns(w[t], *rows))
        r = [lroll(z[t][0], 1) for t in range(2)]
        l = [lroll(z[t][2], -1) for t in range(2)]
        r[1] = jnp.where(head_lane, r[0], r[1])
        l[0] = jnp.where(tail_lane, l[1], l[0])
        return [z[t][1] + (r[t] + l[t]) for t in range(2)], mid

    def finish(b, s, pair, sums):
        j = b * UNROLL + s
        pair, sums = list(pair), list(sums)
        if last:
            group = s // BLOCKS
            strip = st[(s % BLOCKS + 1) * SUB : (s % BLOCKS + 2) * SUB, :]
            pair[0] = jnp.where(lane < 4, lroll(strip, -(GROUP * group + 4)), pair[0])
            pair[1] = jnp.where(lane >= LANES - 4, lroll(strip, 100 - GROUP * group), pair[1])
            out = jnp.concatenate(pair, axis=1) * (1.0 / LOG2E)
            vol_ref[D - 1 - j] = out.astype(jnp.bfloat16)
            done(b * UNROLL + s if isinstance(b, int) else s)
            level = (D - 1 - j).astype(jnp.float32) * (1.0 / D)
        for t in range(2):
            if not last:
                v[t, pl.ds(pl.multiple_of((j + 1) * SUB, SUB), SUB), :] = pair[t]
            e = jnp.exp2(pair[t])
            sums[2 * t] += e
            sums[2 * t + 1] += e * (level if last else e)
        return sums

    def advance(refs, b, s, carry):
        p_prev, s_prev, v_prev, acc = carry
        p, mid = pooled(refs, s)
        s_now = [p_prev[t] + p[t] for t in range(2)]
        new = [keep_own[t] * v_prev[t] + (s_prev[t] + s_now[t]) for t in range(2)]
        before = (b - 1, UNROLL - 1) if s == 0 else (b, s - 1)
        return p, s_now, mid, finish(*before, new, acc)

    def block_refs(b):
        at = pl.ds(pl.multiple_of(b * (UNROLL * SUB), SUB), (UNROLL + 2) * SUB)
        return [v.at[t, at, :] for t in range(2)]

    def loop(b, carry):
        p, s, m, acc = carry
        carry = list(p), list(s), list(m), list(acc)
        refs = block_refs(b)
        for k in range(UNROLL):
            carry = advance(refs, b, k, carry)
        return tuple(tuple(c) for c in carry)

    refs = block_refs(0)
    p, mid = pooled(refs, 0)
    carry = p, [2.0 * x for x in p], mid, [none] * 4
    for k in range(1, UNROLL):
        carry = advance(refs, jnp.int32(0), k, carry)
    carry = tuple(tuple(c) for c in carry)
    p_prev, s_prev, v_prev, acc = lax.fori_loop(1, D // UNROLL, loop, carry)
    new = [keep_own[t] * v_prev[t] + (s_prev[t] + 2.0 * p_prev[t]) for t in range(2)]
    return tuple(finish(jnp.int32(D // UNROLL - 1), UNROLL - 1, new, acc))


def kernel(
    n, left_hbm, right_hbm, mask_hbm, offs_ref, v, st, w_ref, sums_ref, usable_ref,
    left_ref, right_ref, mask_ref,
    high_out, high, low_out, low_in, lf, rf, t4, rhs_ref, part, u, own, edge_w, edge_now, edge_sent, edge_left, edge_right, sent, from_left, from_right, load_sem, send_sem, recv_sem,
):
    channels = left_ref.shape[0]
    tile = left_ref.shape[2]
    me = lax.axis_index("col")
    has_left, has_right = me > 0, me < n - 1
    lane = iota((SUB, LANES), 1)

    barrier = pltpu.get_barrier_semaphore()

    @pl.when(has_right)
    def _():
        pl.semaphore_signal(barrier, inc=1, device_id={"col": me + 1}, device_id_type=MESH)

    @pl.when(has_left)
    def _():
        pl.semaphore_signal(barrier, inc=1, device_id={"col": me - 1}, device_id_type=MESH)

    loads = [
        pltpu.make_async_copy(src, dst, load_sem.at[i])
        for i, (src, dst) in enumerate((
            (right_hbm, right_ref), (left_hbm, left_ref), (mask_hbm, mask_ref)
        ))
    ]
    for load in loads:
        load.start()

    @pl.when(jnp.logical_not(has_left))
    def _():
        high[...] = jnp.zeros(high.shape, high.dtype)
        low_in[...] = jnp.zeros(low_in.shape, low_in.dtype)
        from_left[...] = jnp.zeros(from_left.shape, jnp.float32)
        edge_left[...] = jnp.zeros(edge_left.shape, jnp.float32)

    @pl.when(jnp.logical_not(has_right))
    def _():
        from_right[...] = jnp.zeros(from_right.shape, jnp.float32)
        edge_right[...] = jnp.zeros(edge_right.shape, jnp.float32)

    def remote(src, dst, slot, to):
        return pltpu.make_async_remote_copy(
            src_ref=src, dst_ref=dst, send_sem=send_sem.at[slot], recv_sem=recv_sem.at[slot],
            device_id={"col": to}, device_id_type=MESH,
        )

    halves = [pl.ds(i * SUB // 2, SUB // 2) for i in range(2)]
    high_copies = [remote(high_out.at[h], high.at[h], 2 + i, me + 1) for i, h in enumerate(halves)]
    low_copy = remote(low_out, low_in, 6, me + 1)
    strip_right = remote(sent.at[1], from_left, 0, me + 1)
    strip_left = remote(sent.at[0], from_right, 1, me - 1)
    edge_right_copy = remote(edge_sent.at[1], edge_left, 4, me + 1)
    edge_left_copy = remote(edge_sent.at[0], edge_right, 5, me - 1)

    for load in loads:
        load.wait()

    for c in range(channels):
        for t in range(2):
            rf[t, c * SUB : (c + 1) * SUB, :] = right_ref[c, :, t * LANES : (t + 1) * LANES].astype(jnp.float32)

    def own_row(t, y):
        return rf[t, pl.ds(y, channels, stride=SUB), :]

    wide_lane = iota((channels, LANES), 1)
    for y in range(SUB):
        high_out[y] = own_row(1, y).astype(high_out.dtype)
    for y in range(0, SUB, 2):
        pair = jnp.where(wide_lane < LANES // 2, lroll(own_row(0, y), LANES // 2), own_row(0, y + 1))
        low_out[y // 2] = pair.astype(low_out.dtype)

    usable = mask_ref[...].astype(jnp.float32)
    usable_ref[...] = usable

    for c in range(channels):
        for t in range(2):
            lf[t, c * SUB : (c + 1) * SUB, :] = left_ref[c, :, t * LANES : (t + 1) * LANES].astype(jnp.float32)

    none = jnp.zeros((SUB, LANES), jnp.float32)
    for q in range(channels // PER):
        out = none
        for t in range(2):
            rows = range(q * PER, (q + 1) * PER)
            out = pack([lf[t, c * SUB : (c + 1) * SUB, :] for c in rows], t, out)
        own[BLOCKS + q] = out
    mask_at = BLOCKS + channels // PER
    out = none
    for t in range(2):
        out = pack([usable[:, t * LANES : (t + 1) * LANES]] * PER, t, out)
    own[mask_at] = out
    for q in range(mask_at + 1, own.shape[0]):
        own[q] = none

    place4 = (lane % GROUP) // 4

    def gather(first, target, m):
        for side, at in ((0, 1), (1, 6)):
            out = own[first + 8 * m + at]
            for i in range(8):
                if i != at:
                    out = jnp.where(place4 == i, lroll(own[first + 8 * m + i], 4 * (i - at)), out)
            target[side, m] = out

    for m in range(edge_sent.shape[1]):
        gather(BLOCKS, edge_sent, m)

    pl.semaphore_wait(barrier, has_left.astype(jnp.int32) + has_right.astype(jnp.int32))

    even = me % 2 == 0

    @pl.when(has_left & even)
    def _():
        edge_left_copy.start()

    @pl.when(has_right)
    def _():
        for copy in high_copies:
            copy.start()
        edge_right_copy.start()
        low_copy.start()

    @pl.when(has_left & jnp.logical_not(even))
    def _():
        edge_left_copy.start()

    zero = jnp.zeros((SUB, tile), jnp.float32)

    sums = (zero,) * 5
    for c in range(channels):
        sums = [s + d for s, d in zip(sums, distances(left_ref[c].astype(jnp.float32)))]
    weights = affinity(sums, channels)
    for i, k in enumerate(STEPS):
        w_ref[i] = weights[k]

    def joined(left, right, first, b):
        m, i = divmod(b, 8)
        out = jnp.where(place4 == 0, lroll(left[m], -4 * i), own[first + b])
        return jnp.where(place4 == 7, lroll(right[m], 4 * (7 - i)), out)

    def over_groups(x):
        return (x + lroll(x, GROUP)) + (lroll(x, 2 * GROUP) + lroll(x, 3 * GROUP))

    def edge_weights(left, right):
        sums = (none,) * 5
        for q in range(channels // PER):
            plane = joined(left, right, BLOCKS, q)
            sums = [a + d for a, d in zip(sums, distances(plane))]
        edge = affinity([over_groups(x) for x in sums], channels)
        for i, k in enumerate(STEPS):
            edge_w[i] = lroll(edge[k], k[0])
        edge_w[len(STEPS)] = joined(left, right, BLOCKS, channels // PER)

    def high_row(y):
        return high[y].astype(jnp.float32)

    def low_row(y):
        x = low_in[y // 2].astype(jnp.float32)
        return x if y % 2 else lroll(x, LANES // 2)

    def turn(t, y, now, after):
        block = [now] + [lroll(jnp.where(wide_lane < s, after, now), -s) for s in range(1, 4)]
        t4[y, t * LANES : (t + 1) * LANES, :] = jnp.concatenate(block, axis=0).T

    depth = 8 * channels
    keep = (iota((depth, tile), 0) // channels == iota((depth, tile), 1) % 8).astype(jnp.bfloat16)
    rows_out = tile - 8 + D
    begin = tile - D + 1
    first_cut, second_cut = LANES // 2, D

    def scores_of(y, low, high, width):
        lhs = jnp.concatenate(
            [t4[y, begin + low : begin + high, :], t4[y, begin + 4 + low : begin + 4 + high, :]],
            axis=1,
        ).astype(jnp.bfloat16)
        return jnp.dot(lhs, rhs_ref[y, :, :width], preferred_element_type=jnp.float32)

    def straighten(y, t, x):
        for bit in (64, 32, 16, 8):
            size = x.shape[0] - bit
            on = (iota((size, LANES), 1) // bit) % 2 == 1
            x = jnp.where(on, x[bit:], x[:size])
        u[t, y * PITCH : y * PITCH + D, :] = x

    for y in range(SUB):
        turn(2, y, own_row(0, y), own_row(1, y))
        turn(3, y, own_row(1, y), own_row(1, y))
    for y in range(SUB):
        l_row = jnp.concatenate(
            [lf[t, pl.ds(y, channels, stride=SUB), :] for t in range(2)], axis=1
        ).astype(jnp.bfloat16)
        rhs_ref[y] = jnp.concatenate([l_row] * 8, axis=0) * keep
        part[y, second_cut:, :] = scores_of(y, second_cut, rows_out, tile)

    for i, copy in enumerate(high_copies):
        @pl.when(has_left)
        def _():
            copy.wait_recv()

        rows = range(i * SUB // 2, (i + 1) * SUB // 2)
        for y in rows:
            turn(1, y, high_row(y), own_row(0, y))
        for y in rows:
            part[y, first_cut:second_cut, :] = scores_of(y, first_cut, second_cut, tile)
            straighten(y, 1, part[y, LANES:, LANES:])

    @pl.when(has_left)
    def _():
        low_copy.wait_recv()

    def edges_arrived():
        @pl.when(has_left)
        def _():
            edge_right_copy.wait_recv()

        @pl.when(has_right)
        def _():
            edge_left_copy.wait_recv()

    scale = LOG2E / math.sqrt(channels)
    reach = offs_ref[0] * tile
    for t in range(2):
        v[t, :SUB, :] = none
        v[t, (D + 1) * SUB :, :] = none
    st[:SUB, :] = none
    st[(BLOCKS + 1) * SUB :, :] = none

    @pl.when(even)
    def _():
        edges_arrived()
        edge_now[0] = edge_left[...]
        edge_now[1] = edge_right[...]

    @pl.when(jnp.logical_not(even))
    def _():
        edge_now[...] = jnp.zeros(edge_now.shape, jnp.float32)

    for y in range(SUB):
        turn(0, y, low_row(y), high_row(y))
    edge_weights(edge_now.at[0], edge_now.at[1])
    for y in range(SUB):
        x = scores_of(y, 0, first_cut, LANES)
        straighten(y, 0, jnp.concatenate([x, part[y, first_cut : D + LANES - 8, :LANES]], axis=0))

    @pl.when(me >= 0)
    def _():
        limit = [lane + (reach + t * LANES) for t in range(2)]
        factor = [usable[:, t * LANES : (t + 1) * LANES] * scale for t in range(2)]
        sums = [none] * 4
        for b in range(BLOCKS):
            planes = []
            for s in range(PER):
                j = s * BLOCKS + b
                pair = []
                for t in range(2):
                    corr = u[t, pl.ds(j, SUB, stride=PITCH), :]
                    value = jnp.where(limit[t] >= D - 1 - j, corr, FLOOR_COST * LOG2E / scale) * factor[t]
                    v[t, (j + 1) * SUB : (j + 2) * SUB, :] = value
                    e = jnp.exp2(value)
                    sums[2 * t] += e
                    sums[2 * t + 1] += e * e
                    pair.append(value)
                planes.append(pair)
            out = none
            for t in range(2):
                out = pack([pair[t] for pair in planes], t, out)
            own[b] = out
        for t in range(4):
            sums_ref[t] = sums[t]
        for m in range(sent.shape[1]):
            gather(0, sent, m)

    @pl.when(has_right)
    def _():
        strip_right.start()

    @pl.when(has_left)
    def _():
        strip_left.start()

    sums = lax.fori_loop(
        0, ITERS - 1, lambda i, s: step(v, st, w_ref, usable, None, s),
        tuple(sums_ref[t] for t in range(4)),
    )

    @pl.when(jnp.logical_not(even))
    def _():
        edges_arrived()
        edge_weights(edge_left, edge_right)

    @pl.when(has_left)
    def _():
        strip_right.wait_recv()

    @pl.when(has_right)
    def _():
        strip_left.wait_recv()

    strip_weights = {k: edge_w[i] for i, k in enumerate(STEPS)}
    strip_usable = edge_w[len(STEPS)]

    s1, s2 = none, none
    for b in range(BLOCKS):
        value = joined(from_left, from_right, 0, b)
        st[(b + 1) * SUB : (b + 2) * SUB, :] = value
        e = jnp.exp2(value)
        s1, s2 = s1 + e, s2 + e * e
    lowest, highest = lane < GROUP, lane >= LANES - GROUP

    def strip_step(i, sums):
        gating = gate(over_groups(sums[0]), over_groups(sums[1]))
        keep_own, part = strip_usable * gating, 0.25 * strip_usable * (1.0 - gating)

        def pooled(b):
            rows = three(st, b)
            z = columns(strip_weights, *rows)
            return z[1] + (lroll(z[0], 1) + lroll(z[2], -1)), rows[1]

        p, value = pooled(0)
        p_end, value_end = pooled(BLOCKS - 1)
        pair = p + jnp.where(lowest, p, lroll(p_end, GROUP))
        p_after = jnp.where(highest, p_end, lroll(p, -GROUP))
        s1, s2 = none, none
        for b in range(BLOCKS):
            if b < BLOCKS - 2:
                p_now, value_now = pooled(b + 1)
            elif b == BLOCKS - 2:
                p_now, value_now = p_end, value_end
            else:
                p_now, value_now = p_after, None
            pair_now = p + p_now
            new = keep_own * value + part * (pair + pair_now)
            st[(b + 1) * SUB : (b + 2) * SUB, :] = new
            e = jnp.exp2(new)
            s1, s2 = s1 + e, s2 + e * e
            p, value, pair = p_now, value_now, pair_now
        return s1, s2

    lax.fori_loop(0, ITERS, strip_step, (s1, s2))

    for t in range(4):
        sums_ref[t] = sums[t]

    @pl.when(has_right)
    def _():
        for copy in high_copies:
            copy.wait_send()
        low_copy.wait_send()
        edge_right_copy.wait_send()
        strip_right.wait_send()

    @pl.when(has_left)
    def _():
        edge_left_copy.wait_send()
        strip_left.wait_send()


def last_kernel(usable_ref, v, st, w_ref, sums_ref, disp_hbm, vol_hbm, disp_ref, vol_ref, sem):
    def put(b):
        at = pl.ds(D - (b + 1) * PUT, PUT)
        return pltpu.make_async_copy(vol_ref.at[at], vol_hbm.at[at], sem.at[b])

    def done(j):
        if (j + 1) % PUT == 0:
            put(j // PUT).start()

    out = step(v, st, w_ref, usable_ref[...], vol_ref, [sums_ref[t] for t in range(4)], done)
    for t in range(2):
        disp_ref[:, t * LANES : (t + 1) * LANES] = out[2 * t + 1] / out[2 * t]
    disp = pltpu.make_async_copy(disp_ref, disp_hbm, sem.at[D // PUT])
    disp.start()
    for b in range(D // PUT):
        put(b).wait()
    disp.wait()


def on_device(n, left_features, right_features, tile_offsets, valid_mask):
    channels, rows, tile = left_features.shape
    vmem = pl.BlockSpec(memory_space=pltpu.VMEM)
    hbm = pl.BlockSpec(memory_space=pltpu.HBM)
    edges = -(-(channels // PER + 1) // 8)
    strips = BLOCKS + 8 * edges
    f32 = jnp.float32
    state = pl.pallas_call(
        functools.partial(kernel, n),
        out_shape=(
            jax.ShapeDtypeStruct((2, (D + 2) * SUB, LANES), f32),
            jax.ShapeDtypeStruct(((BLOCKS + 2) * SUB, LANES), f32),
            jax.ShapeDtypeStruct((len(STEPS), SUB, tile), f32),
            jax.ShapeDtypeStruct((4, SUB, LANES), f32),
            jax.ShapeDtypeStruct((SUB, tile), f32),
        ),
        in_specs=[hbm] * 3 + [pl.BlockSpec(memory_space=pltpu.SMEM)],
        out_specs=(vmem,) * 5,
        scratch_shapes=[
            pltpu.VMEM((channels, rows, tile), jnp.bfloat16),
            pltpu.VMEM((channels, rows, tile), jnp.bfloat16),
            pltpu.VMEM((rows, tile), jnp.int32),
            pltpu.VMEM((rows, channels, LANES), jnp.bfloat16),
            pltpu.VMEM((rows, channels, LANES), jnp.bfloat16),
            pltpu.VMEM((rows // 2, channels, LANES), jnp.bfloat16),
            pltpu.VMEM((rows // 2, channels, LANES), jnp.bfloat16),
            pltpu.VMEM((2, channels * SUB, LANES), f32),
            pltpu.VMEM((2, channels * SUB, LANES), f32),
            pltpu.VMEM((SUB, 2 * tile, LANES), f32),
            pltpu.VMEM((SUB, 8 * channels, tile), jnp.bfloat16),
            pltpu.VMEM((SUB, tile - 8 + D, tile), f32),
            pltpu.VMEM((2, SUB * PITCH, LANES), f32),
            pltpu.VMEM((strips, SUB, LANES), f32),
            pltpu.VMEM((len(STEPS) + 1, SUB, LANES), f32),
            pltpu.VMEM((2, edges, SUB, LANES), f32),
            pltpu.VMEM((2, edges, SUB, LANES), f32),
            pltpu.VMEM((edges, SUB, LANES), f32),
            pltpu.VMEM((edges, SUB, LANES), f32),
            pltpu.VMEM((2, BLOCKS // 8, SUB, LANES), f32),
            pltpu.VMEM((BLOCKS // 8, SUB, LANES), f32),
            pltpu.VMEM((BLOCKS // 8, SUB, LANES), f32),
            pltpu.SemaphoreType.DMA((3,)),
            pltpu.SemaphoreType.DMA((7,)),
            pltpu.SemaphoreType.DMA((7,)),
        ],
        compiler_params=pltpu.CompilerParams(
            collective_id=0, has_side_effects=True, vmem_limit_bytes=VMEM_LIMIT
        ),
    )(
        *(pltpu.with_memory_space_constraint(x, pltpu.HBM) for x in (left_features, right_features, valid_mask)),
        tile_offsets,
    )
    v, st, w, sums, usable = state
    return pl.pallas_call(
        last_kernel,
        out_shape=(
            jax.ShapeDtypeStruct((rows, tile), f32),
            jax.ShapeDtypeStruct((D, rows, tile), jnp.bfloat16),
        ),
        in_specs=[vmem] * 5,
        out_specs=(hbm, hbm),
        scratch_shapes=[
            pltpu.VMEM((rows, tile), f32),
            pltpu.VMEM((D, rows, tile), jnp.bfloat16),
            pltpu.SemaphoreType.DMA((D // PUT + 1,)),
        ],
        compiler_params=pltpu.CompilerParams(vmem_limit_bytes=VMEM_LIMIT),
    )(usable, v, st, w, sums)


def solution(mesh):
    return jax.shard_map(
        functools.partial(on_device, mesh.shape["col"]),
        mesh=mesh,
        in_specs=(
            P(None, None, ("groups", "col")),
            P(None, None, ("groups", "col")),
            P(("groups", "col")),
            P(None, ("groups", "col")),
        ),
        out_specs=(P(None, ("groups", "col")), P(None, None, ("groups", "col"))),
        check_vma=False,
    )
```

```python
import functools
import math

import jax
import jax.numpy as jnp
from jax import lax
from jax.experimental import pallas as pl
from jax.experimental.pallas import tpu as pltpu
from jax.sharding import PartitionSpec as P

D = 192
ITERS = 4
FLOOR_COST = -4.0
LANES = 128
SUB = 8
MESH = pl.DeviceIdType.MESH
STEPS = tuple((a, b) for a in (-1, 0, 1) for b in (-1, 0, 1))
PITCH = D + 8
GROUP = 32
PER = LANES // GROUP
BLOCKS = D // PER
LOG2E = math.log2(math.e)
UNROLL = 192
PUT = 16
PIECES = 1
VMEM_LIMIT = 24 * 1024 * 1024


def lroll(x, shift):
    shift = shift % x.shape[-1]
    return x if shift == 0 else pltpu.roll(x, shift, x.ndim - 1)


def sroll(x, shift):
    shift = shift % x.shape[-2]
    return x if shift == 0 else pltpu.roll(x, shift, x.ndim - 2)


def iota(shape, dim):
    return lax.broadcasted_iota(jnp.int32, shape, dim)


def distances(plane):
    right = lroll(plane, -1)
    others = (right, sroll(plane, -1), sroll(right, -1), sroll(lroll(plane, 1), -1))
    return tuple((plane - other) ** 2 for other in others) + (plane * plane,)


def affinity(sums, channels):
    across, down, down_right, down_left, norm = sums
    row = iota(across.shape, 0)
    first, last = row == 0, row == across.shape[0] - 1
    dist = {(1, 0): across, (-1, 0): lroll(across, 1)}
    for a, base in ((1, down_right), (0, down), (-1, down_left)):
        dist[a, 1] = jnp.where(last, norm, base)
        dist[-a, -1] = jnp.where(first, norm, sroll(lroll(base, a), 1))
    e = {k: jnp.exp(-d / (2.0 * channels)) for k, d in dist.items()}
    e[0, 0] = jnp.ones_like(across)
    total = sum(e[k] for k in STEPS)
    out = {k: e[k] / total for k in STEPS}
    for a in (-1, 0, 1):
        out[a, 1] = jnp.where(last, 0.0, out[a, 1])
        out[a, -1] = jnp.where(first, 0.0, out[a, -1])
    return out


def gate(s1, s2):
    purity = D * s2 / (s1 * s1)
    return purity / (1.0 + purity)


def coefficients(weights, usable, s1, s2):
    gating = gate(s1, s2)
    part = 0.25 * usable * (1.0 - gating)
    return {k: lroll(weights[k] * part, k[0]) for k in STEPS}, usable * gating


def columns(w, above, mid, below):
    return [w[a, -1] * above + w[a, 0] * mid + w[a, 1] * below for a in (-1, 0, 1)]


def three(ref, s):
    at = (s + 1) * SUB
    return ref[at - 1 : at - 1 + SUB, :], ref[at : at + SUB, :], ref[at + 1 : at + 1 + SUB, :]


def pack(planes, side, out):
    lane = iota((SUB, LANES), 1)
    place = lane % GROUP
    low, shift = ((4, 4), (16, 16 - 116))[side]
    here = (place >= low) & (place < low + 12)
    for s, plane in enumerate(planes):
        out = jnp.where((lane // GROUP == s) & here, lroll(plane, GROUP * s + shift), out)
    return out


def step(v, st, w_ref, usable, vol_ref, sums, done=None):
    last = vol_ref is not None
    lane = iota((SUB, LANES), 1)
    head_lane, tail_lane = lane == 0, lane == LANES - 1
    none = jnp.zeros((SUB, LANES), jnp.float32)
    wide = lambda a, b: jnp.concatenate([a, b], axis=1)
    w, keep_own = coefficients(
        {k: w_ref[i] for i, k in enumerate(STEPS)}, usable,
        wide(sums[0], sums[2]), wide(sums[1], sums[3]),
    )
    cut = lambda x, t: x[:, t * LANES : (t + 1) * LANES]
    w = [{k: cut(w[k], t) for k in STEPS} for t in range(2)]
    keep_own = [cut(keep_own, t) for t in range(2)]

    def pooled(refs, s):
        z, mid = [], []
        for t in range(2):
            rows = three(refs[t], s)
            mid.append(rows[1])
            z.append(columns(w[t], *rows))
        r = [lroll(z[t][0], 1) for t in range(2)]
        l = [lroll(z[t][2], -1) for t in range(2)]
        r[1] = jnp.where(head_lane, r[0], r[1])
        l[0] = jnp.where(tail_lane, l[1], l[0])
        return [z[t][1] + (r[t] + l[t]) for t in range(2)], mid

    def finish(b, s, pair, sums):
        j = b * UNROLL + s
        pair, sums = list(pair), list(sums)
        if last:
            group = s // BLOCKS
            strip = st[(s % BLOCKS + 1) * SUB : (s % BLOCKS + 2) * SUB, :]
            pair[0] = jnp.where(lane < 4, lroll(strip, -(GROUP * group + 4)), pair[0])
            pair[1] = jnp.where(lane >= LANES - 4, lroll(strip, 100 - GROUP * group), pair[1])
            out = jnp.concatenate(pair, axis=1) * (1.0 / LOG2E)
            vol_ref[D - 1 - j] = out.astype(jnp.bfloat16)
            done(b * UNROLL + s if isinstance(b, int) else s)
            level = (D - 1 - j).astype(jnp.float32) * (1.0 / D)
        for t in range(2):
            if not last:
                v[t, pl.ds(pl.multiple_of((j + 1) * SUB, SUB), SUB), :] = pair[t]
            e = jnp.exp2(pair[t])
            sums[2 * t] += e
            sums[2 * t + 1] += e * (level if last else e)
        return sums

    def advance(refs, b, s, carry):
        p_prev, s_prev, v_prev, acc = carry
        p, mid = pooled(refs, s)
        s_now = [p_prev[t] + p[t] for t in range(2)]
        new = [keep_own[t] * v_prev[t] + (s_prev[t] + s_now[t]) for t in range(2)]
        before = (b - 1, UNROLL - 1) if s == 0 else (b, s - 1)
        return p, s_now, mid, finish(*before, new, acc)

    def block_refs(b):
        at = pl.ds(pl.multiple_of(b * (UNROLL * SUB), SUB), (UNROLL + 2) * SUB)
        return [v.at[t, at, :] for t in range(2)]

    def loop(b, carry):
        p, s, m, acc = carry
        carry = list(p), list(s), list(m), list(acc)
        refs = block_refs(b)
        for k in range(UNROLL):
            carry = advance(refs, b, k, carry)
        return tuple(tuple(c) for c in carry)

    refs = block_refs(0)
    p, mid = pooled(refs, 0)
    carry = p, [2.0 * x for x in p], mid, [none] * 4
    for k in range(1, UNROLL):
        carry = advance(refs, jnp.int32(0), k, carry)
    carry = tuple(tuple(c) for c in carry)
    p_prev, s_prev, v_prev, acc = lax.fori_loop(1, D // UNROLL, loop, carry)
    new = [keep_own[t] * v_prev[t] + (s_prev[t] + 2.0 * p_prev[t]) for t in range(2)]
    return tuple(finish(jnp.int32(D // UNROLL - 1), UNROLL - 1, new, acc))


def kernel(
    n, left_hbm, right_hbm, mask_hbm, offs_ref, v, st, w_ref, sums_ref, usable_ref,
    left_ref, right_ref, mask_ref,
    high_out, high, low_out, low_in, lf, rf, t4, rhs_ref, part, u, own, edge_w, edge_now, edge_sent, edge_left, edge_right, sent, from_left, from_right, load_sem, send_sem, recv_sem,
):
    channels = left_ref.shape[0]
    tile = left_ref.shape[2]
    me = lax.axis_index("col")
    has_left, has_right = me > 0, me < n - 1
    lane = iota((SUB, LANES), 1)

    barrier = pltpu.get_barrier_semaphore()

    @pl.when(has_right)
    def _():
        pl.semaphore_signal(barrier, inc=1, device_id={"col": me + 1}, device_id_type=MESH)

    @pl.when(has_left)
    def _():
        pl.semaphore_signal(barrier, inc=1, device_id={"col": me - 1}, device_id_type=MESH)

    loads = [
        pltpu.make_async_copy(src, dst, load_sem.at[i])
        for i, (src, dst) in enumerate((
            (right_hbm, right_ref), (left_hbm, left_ref), (mask_hbm, mask_ref)
        ))
    ]
    for load in loads:
        load.start()

    @pl.when(jnp.logical_not(has_left))
    def _():
        high[...] = jnp.zeros(high.shape, high.dtype)
        low_in[...] = jnp.zeros(low_in.shape, low_in.dtype)
        from_left[...] = jnp.zeros(from_left.shape, jnp.float32)
        edge_left[...] = jnp.zeros(edge_left.shape, jnp.float32)

    @pl.when(jnp.logical_not(has_right))
    def _():
        from_right[...] = jnp.zeros(from_right.shape, jnp.float32)
        edge_right[...] = jnp.zeros(edge_right.shape, jnp.float32)

    def remote(src, dst, slot, to):
        return pltpu.make_async_remote_copy(
            src_ref=src, dst_ref=dst, send_sem=send_sem.at[slot], recv_sem=recv_sem.at[slot],
            device_id={"col": to}, device_id_type=MESH,
        )

    pieces = [pl.ds(i * SUB // PIECES, SUB // PIECES) for i in range(PIECES)]
    high_copies = [remote(high_out.at[h], high.at[h], 2 + i, me + 1) for i, h in enumerate(pieces)]
    low_copy = remote(low_out, low_in, 6, me + 1)
    strip_right = remote(sent.at[1], from_left, 0, me + 1)
    strip_left = remote(sent.at[0], from_right, 1, me - 1)
    edge_right_copy = remote(edge_sent.at[1], edge_left, 4, me + 1)
    edge_left_copy = remote(edge_sent.at[0], edge_right, 5, me - 1)

    for load in loads:
        load.wait()

    for c in range(channels):
        for t in range(2):
            rf[t, c * SUB : (c + 1) * SUB, :] = right_ref[c, :, t * LANES : (t + 1) * LANES].astype(jnp.float32)

    def own_row(t, y):
        return rf[t, pl.ds(y, channels, stride=SUB), :]

    wide_lane = iota((channels, LANES), 1)
    for y in range(SUB):
        high_out[y] = own_row(1, y).astype(high_out.dtype)
    for y in range(0, SUB, 2):
        pair = jnp.where(wide_lane < LANES // 2, lroll(own_row(0, y), LANES // 2), own_row(0, y + 1))
        low_out[y // 2] = pair.astype(low_out.dtype)

    usable = mask_ref[...].astype(jnp.float32)
    usable_ref[...] = usable

    for c in range(channels):
        for t in range(2):
            lf[t, c * SUB : (c + 1) * SUB, :] = left_ref[c, :, t * LANES : (t + 1) * LANES].astype(jnp.float32)

    none = jnp.zeros((SUB, LANES), jnp.float32)
    for q in range(channels // PER):
        out = none
        for t in range(2):
            rows = range(q * PER, (q + 1) * PER)
            out = pack([lf[t, c * SUB : (c + 1) * SUB, :] for c in rows], t, out)
        own[BLOCKS + q] = out
    mask_at = BLOCKS + channels // PER
    out = none
    for t in range(2):
        out = pack([usable[:, t * LANES : (t + 1) * LANES]] * PER, t, out)
    own[mask_at] = out
    for q in range(mask_at + 1, own.shape[0]):
        own[q] = none

    place4 = (lane % GROUP) // 4

    def gather(first, target, m):
        for side, at in ((0, 1), (1, 6)):
            out = own[first + 8 * m + at]
            for i in range(8):
                if i != at:
                    out = jnp.where(place4 == i, lroll(own[first + 8 * m + i], 4 * (i - at)), out)
            target[side, m] = out

    for m in range(edge_sent.shape[1]):
        gather(BLOCKS, edge_sent, m)

    pl.semaphore_wait(barrier, has_left.astype(jnp.int32) + has_right.astype(jnp.int32))

    even = me % 2 == 0

    @pl.when(has_left & even)
    def _():
        edge_left_copy.start()

    @pl.when(has_right)
    def _():
        for copy in high_copies:
            copy.start()
        edge_right_copy.start()
        low_copy.start()

    @pl.when(has_left & jnp.logical_not(even))
    def _():
        edge_left_copy.start()

    zero = jnp.zeros((SUB, tile), jnp.float32)

    sums = (zero,) * 5
    for c in range(channels):
        sums = [s + d for s, d in zip(sums, distances(left_ref[c].astype(jnp.float32)))]
    weights = affinity(sums, channels)
    for i, k in enumerate(STEPS):
        w_ref[i] = weights[k]

    def joined(left, right, first, b):
        m, i = divmod(b, 8)
        out = jnp.where(place4 == 0, lroll(left[m], -4 * i), own[first + b])
        return jnp.where(place4 == 7, lroll(right[m], 4 * (7 - i)), out)

    def over_groups(x):
        return (x + lroll(x, GROUP)) + (lroll(x, 2 * GROUP) + lroll(x, 3 * GROUP))

    def edge_weights(left, right):
        sums = (none,) * 5
        for q in range(channels // PER):
            plane = joined(left, right, BLOCKS, q)
            sums = [a + d for a, d in zip(sums, distances(plane))]
        edge = affinity([over_groups(x) for x in sums], channels)
        for i, k in enumerate(STEPS):
            edge_w[i] = lroll(edge[k], k[0])
        edge_w[len(STEPS)] = joined(left, right, BLOCKS, channels // PER)

    def high_row(y):
        return high[y].astype(jnp.float32)

    def low_row(y):
        x = low_in[y // 2].astype(jnp.float32)
        return x if y % 2 else lroll(x, LANES // 2)

    def turn(t, y, now, after):
        block = [now] + [lroll(jnp.where(wide_lane < s, after, now), -s) for s in range(1, 4)]
        t4[y, t * LANES : (t + 1) * LANES, :] = jnp.concatenate(block, axis=0).T

    depth = 8 * channels
    keep = (iota((depth, tile), 0) // channels == iota((depth, tile), 1) % 8).astype(jnp.bfloat16)
    rows_out = tile - 8 + D
    begin = tile - D + 1
    first_cut, second_cut = LANES // 2, D

    def scores_of(y, low, high, width):
        lhs = jnp.concatenate(
            [t4[y, begin + low : begin + high, :], t4[y, begin + 4 + low : begin + 4 + high, :]],
            axis=1,
        ).astype(jnp.bfloat16)
        return jnp.dot(lhs, rhs_ref[y, :, :width], preferred_element_type=jnp.float32)

    def straighten(y, t, x):
        for bit in (64, 32, 16, 8):
            size = x.shape[0] - bit
            on = (iota((size, LANES), 1) // bit) % 2 == 1
            x = jnp.where(on, x[bit:], x[:size])
        u[t, y * PITCH : y * PITCH + D, :] = x

    for y in range(SUB):
        turn(2, y, own_row(0, y), own_row(1, y))
        turn(3, y, own_row(1, y), own_row(1, y))
    for y in range(SUB):
        l_row = jnp.concatenate(
            [lf[t, pl.ds(y, channels, stride=SUB), :] for t in range(2)], axis=1
        ).astype(jnp.bfloat16)
        rhs_ref[y] = jnp.concatenate([l_row] * 8, axis=0) * keep
        part[y, second_cut:, :] = scores_of(y, second_cut, rows_out, tile)

    for i, copy in enumerate(high_copies):
        @pl.when(has_left)
        def _():
            copy.wait_recv()

        rows = range(i * SUB // PIECES, (i + 1) * SUB // PIECES)
        for y in rows:
            turn(1, y, high_row(y), own_row(0, y))
        for y in rows:
            part[y, first_cut:second_cut, :] = scores_of(y, first_cut, second_cut, tile)
            straighten(y, 1, part[y, LANES:, LANES:])

    @pl.when(has_left)
    def _():
        low_copy.wait_recv()

    def edges_arrived():
        @pl.when(has_left)
        def _():
            edge_right_copy.wait_recv()

        @pl.when(has_right)
        def _():
            edge_left_copy.wait_recv()

    scale = LOG2E / math.sqrt(channels)
    reach = offs_ref[0] * tile
    for t in range(2):
        v[t, :SUB, :] = none
        v[t, (D + 1) * SUB :, :] = none
    st[:SUB, :] = none
    st[(BLOCKS + 1) * SUB :, :] = none

    @pl.when(even)
    def _():
        edges_arrived()
        edge_now[0] = edge_left[...]
        edge_now[1] = edge_right[...]

    @pl.when(jnp.logical_not(even))
    def _():
        edge_now[...] = jnp.zeros(edge_now.shape, jnp.float32)

    for y in range(SUB):
        turn(0, y, low_row(y), high_row(y))
    edge_weights(edge_now.at[0], edge_now.at[1])
    for y in range(SUB):
        x = scores_of(y, 0, first_cut, LANES)
        straighten(y, 0, jnp.concatenate([x, part[y, first_cut : D + LANES - 8, :LANES]], axis=0))

    @pl.when(me >= 0)
    def _():
        limit = [lane + (reach + t * LANES) for t in range(2)]
        factor = [usable[:, t * LANES : (t + 1) * LANES] * scale for t in range(2)]
        sums = [none] * 4
        for b in range(BLOCKS):
            planes = []
            for s in range(PER):
                j = s * BLOCKS + b
                pair = []
                for t in range(2):
                    corr = u[t, pl.ds(j, SUB, stride=PITCH), :]
                    value = jnp.where(limit[t] >= D - 1 - j, corr, FLOOR_COST * LOG2E / scale) * factor[t]
                    v[t, (j + 1) * SUB : (j + 2) * SUB, :] = value
                    e = jnp.exp2(value)
                    sums[2 * t] += e
                    sums[2 * t + 1] += e * e
                    pair.append(value)
                planes.append(pair)
            out = none
            for t in range(2):
                out = pack([pair[t] for pair in planes], t, out)
            own[b] = out
        for t in range(4):
            sums_ref[t] = sums[t]
        for m in range(sent.shape[1]):
            gather(0, sent, m)

    @pl.when(has_right)
    def _():
        strip_right.start()

    @pl.when(has_left)
    def _():
        strip_left.start()

    sums = lax.fori_loop(
        0, ITERS - 1, lambda i, s: step(v, st, w_ref, usable, None, s),
        tuple(sums_ref[t] for t in range(4)),
    )

    @pl.when(jnp.logical_not(even))
    def _():
        edges_arrived()
        edge_weights(edge_left, edge_right)

    @pl.when(has_left)
    def _():
        strip_right.wait_recv()

    @pl.when(has_right)
    def _():
        strip_left.wait_recv()

    strip_weights = {k: edge_w[i] for i, k in enumerate(STEPS)}
    strip_usable = edge_w[len(STEPS)]

    s1, s2 = none, none
    for b in range(BLOCKS):
        value = joined(from_left, from_right, 0, b)
        st[(b + 1) * SUB : (b + 2) * SUB, :] = value
        e = jnp.exp2(value)
        s1, s2 = s1 + e, s2 + e * e
    lowest, highest = lane < GROUP, lane >= LANES - GROUP

    def strip_step(i, sums):
        gating = gate(over_groups(sums[0]), over_groups(sums[1]))
        keep_own, part = strip_usable * gating, 0.25 * strip_usable * (1.0 - gating)

        def pooled(b):
            rows = three(st, b)
            z = columns(strip_weights, *rows)
            return z[1] + (lroll(z[0], 1) + lroll(z[2], -1)), rows[1]

        p, value = pooled(0)
        p_end, value_end = pooled(BLOCKS - 1)
        pair = p + jnp.where(lowest, p, lroll(p_end, GROUP))
        p_after = jnp.where(highest, p_end, lroll(p, -GROUP))
        s1, s2 = none, none
        for b in range(BLOCKS):
            if b < BLOCKS - 2:
                p_now, value_now = pooled(b + 1)
            elif b == BLOCKS - 2:
                p_now, value_now = p_end, value_end
            else:
                p_now, value_now = p_after, None
            pair_now = p + p_now
            new = keep_own * value + part * (pair + pair_now)
            st[(b + 1) * SUB : (b + 2) * SUB, :] = new
            e = jnp.exp2(new)
            s1, s2 = s1 + e, s2 + e * e
            p, value, pair = p_now, value_now, pair_now
        return s1, s2

    lax.fori_loop(0, ITERS, strip_step, (s1, s2))

    for t in range(4):
        sums_ref[t] = sums[t]

    @pl.when(has_right)
    def _():
        for copy in high_copies:
            copy.wait_send()
        low_copy.wait_send()
        edge_right_copy.wait_send()
        strip_right.wait_send()

    @pl.when(has_left)
    def _():
        edge_left_copy.wait_send()
        strip_left.wait_send()


def last_kernel(usable_ref, v, st, w_ref, sums_ref, disp_hbm, vol_hbm, disp_ref, vol_ref, sem):
    def put(b):
        at = pl.ds(D - (b + 1) * PUT, PUT)
        return pltpu.make_async_copy(vol_ref.at[at], vol_hbm.at[at], sem.at[b])

    def done(j):
        if (j + 1) % PUT == 0:
            put(j // PUT).start()

    out = step(v, st, w_ref, usable_ref[...], vol_ref, [sums_ref[t] for t in range(4)], done)
    for t in range(2):
        disp_ref[:, t * LANES : (t + 1) * LANES] = out[2 * t + 1] / out[2 * t]
    disp = pltpu.make_async_copy(disp_ref, disp_hbm, sem.at[D // PUT])
    disp.start()
    for b in range(D // PUT):
        put(b).wait()
    disp.wait()


def on_device(n, left_features, right_features, tile_offsets, valid_mask):
    channels, rows, tile = left_features.shape
    vmem = pl.BlockSpec(memory_space=pltpu.VMEM)
    hbm = pl.BlockSpec(memory_space=pltpu.HBM)
    edges = -(-(channels // PER + 1) // 8)
    strips = BLOCKS + 8 * edges
    f32 = jnp.float32
    state = pl.pallas_call(
        functools.partial(kernel, n),
        out_shape=(
            jax.ShapeDtypeStruct((2, (D + 2) * SUB, LANES), f32),
            jax.ShapeDtypeStruct(((BLOCKS + 2) * SUB, LANES), f32),
            jax.ShapeDtypeStruct((len(STEPS), SUB, tile), f32),
            jax.ShapeDtypeStruct((4, SUB, LANES), f32),
            jax.ShapeDtypeStruct((SUB, tile), f32),
        ),
        in_specs=[hbm] * 3 + [pl.BlockSpec(memory_space=pltpu.SMEM)],
        out_specs=(vmem,) * 5,
        scratch_shapes=[
            pltpu.VMEM((channels, rows, tile), jnp.bfloat16),
            pltpu.VMEM((channels, rows, tile), jnp.bfloat16),
            pltpu.VMEM((rows, tile), jnp.int32),
            pltpu.VMEM((rows, channels, LANES), jnp.bfloat16),
            pltpu.VMEM((rows, channels, LANES), jnp.bfloat16),
            pltpu.VMEM((rows // 2, channels, LANES), jnp.bfloat16),
            pltpu.VMEM((rows // 2, channels, LANES), jnp.bfloat16),
            pltpu.VMEM((2, channels * SUB, LANES), f32),
            pltpu.VMEM((2, channels * SUB, LANES), f32),
            pltpu.VMEM((SUB, 2 * tile, LANES), f32),
            pltpu.VMEM((SUB, 8 * channels, tile), jnp.bfloat16),
            pltpu.VMEM((SUB, tile - 8 + D, tile), f32),
            pltpu.VMEM((2, SUB * PITCH, LANES), f32),
            pltpu.VMEM((strips, SUB, LANES), f32),
            pltpu.VMEM((len(STEPS) + 1, SUB, LANES), f32),
            pltpu.VMEM((2, edges, SUB, LANES), f32),
            pltpu.VMEM((2, edges, SUB, LANES), f32),
            pltpu.VMEM((edges, SUB, LANES), f32),
            pltpu.VMEM((edges, SUB, LANES), f32),
            pltpu.VMEM((2, BLOCKS // 8, SUB, LANES), f32),
            pltpu.VMEM((BLOCKS // 8, SUB, LANES), f32),
            pltpu.VMEM((BLOCKS // 8, SUB, LANES), f32),
            pltpu.SemaphoreType.DMA((3,)),
            pltpu.SemaphoreType.DMA((7,)),
            pltpu.SemaphoreType.DMA((7,)),
        ],
        compiler_params=pltpu.CompilerParams(
            collective_id=0, has_side_effects=True, vmem_limit_bytes=VMEM_LIMIT
        ),
    )(
        *(pltpu.with_memory_space_constraint(x, pltpu.HBM) for x in (left_features, right_features, valid_mask)),
        tile_offsets,
    )
    v, st, w, sums, usable = state
    return pl.pallas_call(
        last_kernel,
        out_shape=(
            jax.ShapeDtypeStruct((rows, tile), f32),
            jax.ShapeDtypeStruct((D, rows, tile), jnp.bfloat16),
        ),
        in_specs=[vmem] * 5,
        out_specs=(hbm, hbm),
        scratch_shapes=[
            pltpu.VMEM((rows, tile), f32),
            pltpu.VMEM((D, rows, tile), jnp.bfloat16),
            pltpu.SemaphoreType.DMA((D // PUT + 1,)),
        ],
        compiler_params=pltpu.CompilerParams(vmem_limit_bytes=VMEM_LIMIT),
    )(usable, v, st, w, sums)


def solution(mesh):
    return jax.shard_map(
        functools.partial(on_device, mesh.shape["col"]),
        mesh=mesh,
        in_specs=(
            P(None, None, ("groups", "col")),
            P(None, None, ("groups", "col")),
            P(("groups", "col")),
            P(None, ("groups", "col")),
        ),
        out_specs=(P(None, ("groups", "col")), P(None, None, ("groups", "col"))),
        check_vma=False,
    )
```
